512 devices in a mesh: ao: 32 (over x, z), ri: 16 (over y, core).
Axes of the slice: x: 4, y: 8, z: 8, core: 2. Of those that a mesh axis runs over, the one named last changes fastest.
Arguments:
- three_center: bfloat16 [256, 12288, 128], P('ri', 'ao'), may hold values from -0.19921875 to 0.19921875
- occ_band: bfloat16 [4096, 640], P('ao'), may hold values from -0.3125 to 0.3125
- virt_band: bfloat16 [4096, 384], P('ao'), may hold values from -0.3125 to 0.3125
- three_mask: int32 [32, 3], P('ao'), may hold values 0 or 1
- occ_mask: int32 [32, 5], P('ao'), may hold values 0 or 1
- virt_mask: int32 [32, 3], P('ao'), may hold values 0 or 1
Outputs:
- chi: float32 [256, 256], P('ri')
The draws below stay inside these ranges and needn't reach their ends.
All inputs are finite; a program needn't handle non-finite values. No bound on the sum of `three_mask` or of `occ_mask` or of `virt_mask` on one device may be relied on, other than what follows from the above.
Results may differ from the reference program's by a relative error of at most 0.004.
Values may be sent and summed in bfloat16 or wider, within the bound.
A program may use at most 64 MiB of HBM per device.

```python
import jax
import jax.numpy as jnp
from jax import lax

TILE = 128
PT = 256
NT = 32


def plant(result, key, smallest, high):
    dims = result.shape
    spot = [jax.random.randint(jax.random.fold_in(key, axis), (), 0, dims[axis]) for axis in range(len(dims))]
    result = result.at[tuple(spot)].set(smallest)
    longest = dims.index(max(dims))
    spot[longest] = (spot[longest] + 1) % dims[longest]
    return result.at[tuple(spot)].set(high)


def steps_of(rng, dims, cuts, low, largest):
    loudness, own = 1.0, jax.random.fold_in(rng, 6)
    for axis_at, blocks in cuts:
        draws = jnp.exp(jax.random.uniform(jax.random.fold_in(own, axis_at), (blocks,), jnp.float32, low / len(cuts), largest / len(cuts)))
        loudness = loudness * jnp.repeat(draws, dims[axis_at] // blocks).reshape([-1 if axis == axis_at else 1 for axis in range(len(dims))])
    return loudness


def normal_values(own_key, shape, scale, limit, split=(), kind=jnp.bfloat16):
    level = steps_of(own_key, shape, split, -0.22, 0.18) if split else 1.0
    drawn = jax.random.normal(own_key, shape, jnp.float32) * scale * level
    return jnp.minimum(jnp.maximum(drawn, -limit), limit).astype(kind)


def setup_inputs(seed: int = 0) -> dict:
    keys = jax.random.split(jax.random.key(seed), 7)
    three_center = normal_values(keys[0], (PT, NT * 3 * TILE, TILE), 0.03, 0.19921875, ((0, 16), (1, 32)))
    occ_band = normal_values(keys[1], (NT * TILE, 5 * TILE), (3 * TILE) ** -0.5, 0.3125, ((0, 32),))
    virt_band = normal_values(keys[2], (NT * TILE, 3 * TILE), (3 * TILE) ** -0.5, 0.3125, ((0, 32),))
    three_mask = plant((jax.random.randint(keys[3], (NT, 3), 0, 4) < 3).astype(jnp.int32), jax.random.fold_in(keys[3], 1), 0, 1)
    occ_mask = plant((jax.random.randint(keys[4], (NT, 5), 0, 4) < 3).astype(jnp.int32), jax.random.fold_in(keys[4], 1), 0, 1)
    virt_mask = plant((jax.random.randint(keys[5], (NT, 3), 0, 4) < 3).astype(jnp.int32), jax.random.fold_in(keys[5], 1), 0, 1)
    return dict(three_center=three_center, occ_band=occ_band, virt_band=virt_band, three_mask=three_mask, occ_mask=occ_mask, virt_mask=virt_mask)


def reference(three_center, occ_band, virt_band, three_mask, occ_mask, virt_mask):
    tile_size = TILE
    tiles = NT
    batch = three_center.shape[0]
    live_b = three_center.reshape(batch, tiles, 3, tile_size, tile_size) * three_mask.astype(three_center.dtype)[None, :, :, None, None]
    live_occ = (occ_band.reshape(tiles, tile_size, 5, tile_size) * occ_mask.astype(occ_band.dtype)[:, None, :, None]).reshape(tiles, tile_size, 5 * tile_size)
    live_virt = (virt_band.reshape(tiles, tile_size, 3, tile_size) * virt_mask.astype(virt_band.dtype)[:, None, :, None]).reshape(tiles, tile_size, 3 * tile_size)
    blank = jnp.zeros((tile_size, tile_size), occ_band.dtype)

    def build_m(index):
        first = jnp.take(live_occ, ((index - 1) % tiles).astype(jnp.int32), axis=0)
        middle = jnp.take(live_occ, index.astype(jnp.int32), axis=0)
        last = jnp.take(live_occ, ((index + 1) % tiles).astype(jnp.int32), axis=0)
        green_block = jnp.concatenate([
            jnp.concatenate([first[:, tile_size:], blank], 1),
            middle,
            jnp.concatenate([blank, last[:, :4 * tile_size]], 1)], 0)
        own_b = jnp.take(live_b, index.astype(jnp.int32), axis=1).reshape(batch, 3 * tile_size, tile_size)
        contracted = jnp.einsum("ml,pmn->pln", green_block.astype(jnp.float32), own_b.astype(jnp.float32))
        return contracted.astype(jnp.bfloat16)

    indices = jnp.arange(tiles, dtype=jnp.int32)
    m_all = lax.map(build_m, indices)

    def add_chi(total, index):
        left = jnp.take(m_all, ((index - 1) % tiles).astype(jnp.int32), axis=0)[:, 2 * tile_size:5 * tile_size]
        own = jnp.take(m_all, index.astype(jnp.int32), axis=0)[:, tile_size:4 * tile_size]
        right = jnp.take(m_all, ((index + 1) % tiles).astype(jnp.int32), axis=0)[:, 0:3 * tile_size]
        needed = jnp.concatenate([left, own, right], 2)
        virt_rows = jnp.take(live_virt, index.astype(jnp.int32), axis=0)
        product = jnp.einsum("plv,sv->pls", needed.astype(jnp.float32), virt_rows.astype(jnp.float32)).astype(jnp.bfloat16)
        own_b = jnp.take(live_b, index.astype(jnp.int32), axis=1).reshape(batch, -1)
        part = jnp.dot(product.reshape(batch, -1), own_b.T, preferred_element_type=jnp.float32)
        return total + part, None

    total, _ = lax.scan(add_chi, jnp.zeros((batch, batch), jnp.float32), indices)
    return -total
```

```python
import functools

import jax
import jax.numpy as jnp
from jax import lax
from jax.experimental import pallas as pl
from jax.experimental.pallas import tpu as pltpu
from jax.sharding import PartitionSpec as P

MESH = pl.DeviceIdType.MESH
F32 = jnp.float32
BF16 = jnp.bfloat16


def kernel(
    n_ao, n_ri, n_x, n_z, tile, rows,
    b_ref, occ_ref, virt_ref, tm_ref, om_ref, vm_ref, o_ref,
    wide, bt, occ_own, occ_left, occ_right, green, virt, m_buf, m_left, m_right,
    nt, b_all, n_all, acc, panels, own_x, own_z,
    occ_ss, occ_rs, m_ss, m_rs, b_ss, b_rs, n_ss, n_rs, p_ss, p_rs, x_ss, x_rs, z_ss, z_rs,
):
    ao = lax.axis_index("ao")
    ri = lax.axis_index("ri")
    x, z = ao // n_z, lax.rem(ao, n_z)
    right, left = lax.rem(ao + 1, n_ao), lax.rem(ao + n_ao - 1, n_ao)
    share = tile // n_ri

    def remote(src, dst, ss, rs, where):
        return pltpu.make_async_remote_copy(
            src_ref=src, dst_ref=dst, send_sem=ss, recv_sem=rs, device_id=where, device_id_type=MESH
        )

    def ri_peer(d):
        return lax.rem(ri + d, n_ri)

    def x_peer(d):
        return lax.rem(x + d, n_x) * n_z + z

    def z_peer(d):
        return x * n_z + lax.rem(z + d, n_z)

    barrier = pltpu.get_barrier_semaphore()

    def greet(where):
        pl.semaphore_signal(barrier, inc=1, device_id=where, device_id_type=MESH)

    greet({"ao": right})
    greet({"ao": left})

    def greet_ri(d, carry):
        greet({"ri": ri_peer(d)})
        return carry

    lax.fori_loop(1, n_ri, greet_ri, 0)
    for d in range(1, n_z):
        greet({"ao": z_peer(d)})
    for d in range(1, n_x):
        greet({"ao": x_peer(d)})

    for j in range(5):
        cols = pl.ds(j * tile, tile)
        occ_own[:, cols] = (occ_ref[:, cols].astype(F32) * om_ref[0, j].astype(F32)).astype(BF16)
    for j in range(3):
        cols = pl.ds(j * tile, tile)
        virt[:, cols] = (virt_ref[:, cols].astype(F32) * vm_ref[0, j].astype(F32)).astype(BF16)

    def regroup(source_rows, stride, target, lam0):
        def body(l, carry):
            target[lam0 + l] = source_rows[pl.ds(l, rows, stride=stride), :].astype(BF16)
            return carry

        lax.fori_loop(0, tile, body, 0, unroll=8)

    def widen_b(j):
        flag = tm_ref[0, j].astype(F32)

        def body(p, carry):
            wide[pl.ds(pl.multiple_of(p * tile, tile), tile), :] = (
                b_ref[p, pl.ds(j * tile, tile), :].astype(F32) * flag
            )
            return carry

        lax.fori_loop(0, rows, body, 0)

    widen_b(0)
    regroup(wide, tile, bt, 0)

    pl.semaphore_wait(barrier, 2 + n_ri - 1 + n_z - 1 + n_x - 1)

    to_right = remote(occ_own.at[:, pl.ds(tile, 4 * tile)], occ_left, occ_ss.at[0], occ_rs.at[0], {"ao": right})
    to_left = remote(occ_own.at[:, pl.ds(0, 4 * tile)], occ_right, occ_ss.at[1], occ_rs.at[1], {"ao": left})
    to_right.start()
    to_left.start()

    def share_copy(source, target, ss, rs, j, d):
        peer = ri_peer(d)
        return remote(
            source.at[pl.ds(pl.multiple_of(j * tile + peer * share, share), share)],
            target.at[j, ri],
            ss.at[j, d],
            rs.at[j, d],
            {"ri": peer},
        )

    def spread(source, target, ss, rs, j):
        def body(d, carry):
            share_copy(source, target, ss, rs, j, d).start()
            return carry

        lax.fori_loop(1, n_ri, body, 0)
        target[j, ri] = source[pl.ds(pl.multiple_of(j * tile + ri * share, share), share)]

    def arrive(source, target, ss, rs, j):
        def body(d, carry):
            share_copy(source, target, ss, rs, j, d).wait_recv()
            return carry

        lax.fori_loop(1, n_ri, body, 0)

    def drain(source, target, ss, rs, j):
        def body(d, carry):
            share_copy(source, target, ss, rs, j, d).wait_send()
            return carry

        lax.fori_loop(1, n_ri, body, 0)

    spread(bt, b_all, b_ss, b_rs, 0)

    to_right.wait_recv()
    to_left.wait_recv()
    for i, (band, shift) in enumerate(((occ_left, 0), (occ_own, 0), (occ_right, -1))):
        flag = tm_ref[0, i].astype(F32)
        for j in range(5):
            k = j + shift
            if 0 <= k < band.shape[1] // tile:
                block = band[:, pl.ds(k * tile, tile)].astype(F32) * flag
                green[pl.ds(j * tile, tile), pl.ds(i * tile, tile)] = block.T.astype(BF16)
            else:
                green[pl.ds(j * tile, tile), pl.ds(i * tile, tile)] = jnp.zeros((tile, tile), BF16)

    def make_m(first, count):
        lhs_rows = pl.ds(first * tile, count * tile)

        def body(q, carry):
            pair = jnp.concatenate([b_ref[2 * q], b_ref[2 * q + 1]], axis=1)
            got = jnp.dot(green[lhs_rows, :], pair, preferred_element_type=F32).astype(BF16)
            m_buf[2 * q, lhs_rows, :] = got[:, :tile]
            m_buf[2 * q + 1, lhs_rows, :] = got[:, tile:]
            return carry

        lax.fori_loop(0, rows // 2, body, 0)

    def m_copies(j):
        cols = pl.ds(j * tile, tile)
        return (
            remote(m_buf.at[:, pl.ds((j + 2) * tile, tile), :], m_left.at[:, cols, :], m_ss.at[0, j], m_rs.at[0, j], {"ao": right}),
            remote(m_buf.at[:, cols, :], m_right.at[:, cols, :], m_ss.at[1, j], m_rs.at[1, j], {"ao": left}),
        )

    make_m(0, 3)
    for copy in m_copies(0):
        copy.start()
    make_m(3, 1)
    for copy in m_copies(1):
        copy.start()
    make_m(4, 1)
    for copy in m_copies(2):
        copy.start()

    for j in (1, 2):
        widen_b(j)
        regroup(wide, tile, bt, j * tile)
        spread(bt, b_all, b_ss, b_rs, j)

    for j in range(3):
        for copy in m_copies(j):
            copy.wait_recv()

        def n_body(p, carry, j=j):
            needed = jnp.concatenate(
                [
                    m_left[p, pl.ds(j * tile, tile), :],
                    m_buf[p, pl.ds((j + 1) * tile, tile), :],
                    m_right[p, pl.ds(j * tile, tile), :],
                ],
                axis=1,
            )
            wide[pl.ds(pl.multiple_of(p * tile, tile), tile), :] = lax.dot_general(
                needed, virt[...], (((1,), (1,)), ((), ())), preferred_element_type=F32
            )
            return carry

        lax.fori_loop(0, rows, n_body, 0)
        regroup(wide, tile, nt, j * tile)
        spread(nt, n_all, n_ss, n_rs, j)

    acc[...] = jnp.zeros_like(acc)
    for j in range(3):
        arrive(bt, b_all, b_ss, b_rs, j)
        arrive(nt, n_all, n_ss, n_rs, j)
        total = acc[...]
        for l in range(0, share, 2):
            size = n_ri * rows

            def pair_of(ref):
                return jnp.concatenate(
                    [ref[j, :, l].reshape(size, tile), ref[j, :, l + 1].reshape(size, tile)], axis=1
                )

            total = total + lax.dot_general(
                pair_of(n_all), pair_of(b_all), (((1,), (1,)), ((), ())), preferred_element_type=F32
            )
        acc[...] = total

    def panel_rows(r):
        return pl.ds(pl.multiple_of(r * rows, rows), rows)

    def panel_copy(d):
        peer = ri_peer(d)
        return remote(acc.at[panel_rows(peer)], panels.at[ri], p_ss.at[d], p_rs.at[d], {"ri": peer})

    def send_panel(d, carry):
        panel_copy(d).start()
        return carry

    lax.fori_loop(1, n_ri, send_panel, 0)
    panels[ri] = acc[panel_rows(ri), :]

    def take_panel(d, carry):
        panel_copy(d).wait_recv()
        return carry

    lax.fori_loop(1, n_ri, take_panel, 0)
    own_x[x] = jnp.sum(panels[...], axis=0)
    x_copies = [remote(own_x.at[x], own_x.at[x], x_ss.at[d], x_rs.at[d], {"ao": x_peer(d)}) for d in range(1, n_x)]
    for copy in x_copies:
        copy.start()
    for copy in x_copies:
        copy.wait_recv()
    own_z[z] = jnp.sum(own_x[...], axis=0)
    z_copies = [remote(own_z.at[z], own_z.at[z], z_ss.at[d], z_rs.at[d], {"ao": z_peer(d)}) for d in range(1, n_z)]
    for copy in z_copies:
        copy.start()
    for copy in z_copies:
        copy.wait_recv()
    o_ref[...] = -jnp.sum(own_z[...], axis=0)

    to_right.wait_send()
    to_left.wait_send()
    for j in range(3):
        for copy in m_copies(j):
            copy.wait_send()
        drain(bt, b_all, b_ss, b_rs, j)
        drain(nt, n_all, n_ss, n_rs, j)

    def sent_panel(d, carry):
        panel_copy(d).wait_send()
        return carry

    lax.fori_loop(1, n_ri, sent_panel, 0)
    for copy in x_copies + z_copies:
        copy.wait_send()


def solution(mesh):
    n_ao, n_ri = mesh.shape["ao"], mesh.shape["ri"]
    n_z = 8
    n_x = n_ao // n_z

    def per_device(three_center, occ_band, virt_band, three_mask, occ_mask, virt_mask):
        rows = three_center.shape[0]
        tile = occ_band.shape[0]
        share = tile // n_ri
        size = n_ri * rows
        dma = pltpu.SemaphoreType.DMA
        vmem = pl.BlockSpec(memory_space=pltpu.VMEM)
        smem = pl.BlockSpec(memory_space=pltpu.SMEM)
        return pl.pallas_call(
            functools.partial(kernel, n_ao, n_ri, n_x, n_z, tile, rows),
            out_shape=jax.ShapeDtypeStruct((rows, size), F32),
            in_specs=[vmem, vmem, vmem, smem, smem, smem],
            out_specs=vmem,
            scratch_shapes=[
                pltpu.VMEM((rows * tile, tile), F32),
                pltpu.VMEM((3 * tile, rows, tile), BF16),
                pltpu.VMEM((tile, 5 * tile), BF16),
                pltpu.VMEM((tile, 4 * tile), BF16),
                pltpu.VMEM((tile, 4 * tile), BF16),
                pltpu.VMEM((5 * tile, 3 * tile), BF16),
                pltpu.VMEM((tile, 3 * tile), BF16),
                pltpu.VMEM((rows, 5 * tile, tile), BF16),
                pltpu.VMEM((rows, 3 * tile, tile), BF16),
                pltpu.VMEM((rows, 3 * tile, tile), BF16),
                pltpu.VMEM((3 * tile, rows, tile), BF16),
                pltpu.VMEM((3, n_ri, share, rows, tile), BF16),
                pltpu.VMEM((3, n_ri, share, rows, tile), BF16),
                pltpu.VMEM((size, size), F32),
                pltpu.VMEM((n_ri, rows, size), F32),
                pltpu.VMEM((n_x, rows, size), F32),
                pltpu.VMEM((n_z, rows, size), F32),
                dma((2,)), dma((2,)),
                dma((2, 3)), dma((2, 3)),
                dma((3, n_ri)), dma((3, n_ri)),
                dma((3, n_ri)), dma((3, n_ri)),
                dma((n_ri,)), dma((n_ri,)),
                dma((n_x,)), dma((n_x,)),
                dma((n_z,)), dma((n_z,)),
            ],
            compiler_params=pltpu.CompilerParams(
                collective_id=0, has_side_effects=True, vmem_limit_bytes=48 * 1024 * 1024
            ),
        )(three_center, occ_band, virt_band, three_mask, occ_mask, virt_mask)

    return jax.shard_map(
        per_device,
        mesh=mesh,
        in_specs=(P("ri", "ao", None), P("ao", None), P("ao", None), P("ao", None), P("ao", None), P("ao", None)),
        out_specs=P("ri", None),
        check_vma=False,
    )
```

```python
import functools

import jax
import jax.numpy as jnp
from jax import lax
from jax.experimental import pallas as pl
from jax.experimental.pallas import tpu as pltpu
from jax.sharding import PartitionSpec as P

MESH = pl.DeviceIdType.MESH
F32 = jnp.float32
BF16 = jnp.bfloat16


def kernel(
    n_ao, n_ri, n_x, n_z, tile, rows,
    b_hbm, occ_hbm, virt_hbm, tm_hbm, om_hbm, vm_hbm, o_ref,
    b_ref, occ_ref, virt_ref, tm_ref, om_ref, vm_ref,
    wide, bt, occ_own, occ_left, occ_right, green, virt, m_buf, m_left, m_right,
    nt, b_all, n_all, acc, panels, own_x, own_z,
    in_sem, occ_ss, occ_rs, m_ss, m_rs, b_ss, b_rs, f_ss, f_rs, n_ss, n_rs, p_ss, p_rs, x_ss, x_rs, z_ss, z_rs,
):
    ao = lax.axis_index("ao")
    ri = lax.axis_index("ri")
    x, z = ao // n_z, lax.rem(ao, n_z)
    y, core = ri // 2, lax.rem(ri, 2)
    n_y = n_ri // 2
    half = n_ri // 2
    side = ri // half
    right, left = lax.rem(ao + 1, n_ao), lax.rem(ao + n_ao - 1, n_ao)
    share = tile // n_ri
    wider = 2 * share

    def far_first(i):
        step = (i + 1) // 2
        return n_y // 2 + step - 2 * step * lax.rem(i, 2)

    def remote(src, dst, ss, rs, where):
        return pltpu.make_async_remote_copy(
            src_ref=src, dst_ref=dst, send_sem=ss, recv_sem=rs, device_id=where, device_id_type=MESH
        )

    def ri_peer(d):
        return lax.rem(ri + d, n_ri)

    def x_peer(d):
        return lax.rem(x + d, n_x) * n_z + z

    def z_peer(d):
        return x * n_z + lax.rem(z + d, n_z)

    b_in = [
        pltpu.make_async_copy(
            b_hbm.at[:, pl.ds(j * tile, tile), :], b_ref.at[:, pl.ds(j * tile, tile), :], in_sem.at[j]
        )
        for j in range(3)
    ]
    small_in = [
        pltpu.make_async_copy(source, target, in_sem.at[3 + i])
        for i, (source, target) in enumerate(
            ((tm_hbm, tm_ref), (om_hbm, om_ref), (vm_hbm, vm_ref), (occ_hbm, occ_ref), (virt_hbm, virt_ref))
        )
    ]
    b_in[0].start()
    for copy in small_in:
        copy.start()
    b_in[1].start()
    b_in[2].start()

    barrier = pltpu.get_barrier_semaphore()

    def greet(where):
        pl.semaphore_signal(barrier, inc=1, device_id=where, device_id_type=MESH)

    greet({"ao": right})
    greet({"ao": left})

    def greet_ri(d, carry):
        greet({"ri": ri_peer(d)})
        return carry

    lax.fori_loop(1, n_ri, greet_ri, 0)
    for d in range(1, n_z):
        greet({"ao": z_peer(d)})
    for d in range(1, n_x):
        greet({"ao": x_peer(d)})

    for copy in small_in:
        copy.wait()
    for j in range(5):
        cols = pl.ds(j * tile, tile)
        occ_own[:, cols] = (occ_ref[:, cols].astype(F32) * om_ref[0, j].astype(F32)).astype(BF16)
    for j in range(3):
        cols = pl.ds(j * tile, tile)
        virt[:, cols] = (virt_ref[:, cols].astype(F32) * vm_ref[0, j].astype(F32)).astype(BF16)

    def regroup(source_rows, stride, target, lam0):
        def body(l, carry):
            target[lam0 + l] = source_rows[pl.ds(l, rows, stride=stride), :].astype(BF16)
            return carry

        lax.fori_loop(0, tile, body, 0, unroll=8)

    def widen_b(j):
        flag = tm_ref[0, j].astype(F32)

        def body(p, carry):
            wide[pl.ds(pl.multiple_of(p * tile, tile), tile), :] = (
                b_ref[p, pl.ds(j * tile, tile), :].astype(F32) * flag
            )
            return carry

        lax.fori_loop(0, rows, body, 0)

    b_in[0].wait()
    widen_b(0)
    regroup(wide, tile, bt, 0)

    pl.semaphore_wait(barrier, 2 + n_ri - 1 + n_z - 1 + n_x - 1)

    to_right = remote(occ_own.at[:, pl.ds(tile, 4 * tile)], occ_left, occ_ss.at[0], occ_rs.at[0], {"ao": right})
    to_left = remote(occ_own.at[:, pl.ds(0, 4 * tile)], occ_right, occ_ss.at[1], occ_rs.at[1], {"ao": left})
    to_right.start()
    to_left.start()

    def b_copy(j, i):
        peer = lax.rem(y + far_first(i // 2), n_y) * 2 + lax.rem(core + 1 + i, 2)
        return remote(
            bt.at[pl.ds(pl.multiple_of(j * tile + peer * share, share), share)],
            b_all.at[j, core_of(peer), ri],
            b_ss.at[j, i],
            b_rs.at[j, ri],
            {"ri": peer},
        )

    def core_of(peer):
        return lax.rem(peer, 2)

    def spread_b(j):
        def body(i, carry):
            b_copy(j, i).start()
            return carry

        lax.fori_loop(0, n_ri - 1, body, 0)
        b_all[j, core, ri] = bt[pl.ds(pl.multiple_of(j * tile + ri * share, share), share)]

    def b_arrive(j):
        def body(d, carry):
            source = ri_peer(d)
            remote(
                bt.at[pl.ds(0, share)], b_all.at[j, core, source], b_ss.at[j, 0], b_rs.at[j, source], {"ri": source}
            ).wait_recv()
            return carry

        lax.fori_loop(1, n_ri, body, 0)

    def b_drain(j):
        def body(i, carry):
            b_copy(j, i).wait_send()
            return carry

        lax.fori_loop(0, n_ri - 1, body, 0)

    def forward(j):
        return remote(b_all.at[j, core], b_all.at[j, core], f_ss.at[j], f_rs.at[j], {"ri": y * 2 + 1 - core})

    def forwarded(j):
        return remote(b_all.at[j, 1 - core], b_all.at[j, 1 - core], f_ss.at[j], f_rs.at[j], {"ri": y * 2 + 1 - core})

    def n_copy(j, i):
        chip = lax.rem(y + far_first(i), n_y)
        return remote(
            nt.at[pl.ds(pl.multiple_of(j * tile + chip * wider, wider), wider)],
            n_all.at[j, lax.rem(ri, half)],
            n_ss.at[j, i],
            n_rs.at[j, lax.rem(ri, half)],
            {"ri": chip * 2 + side},
        )

    def spread_n(j):
        def body(i, carry):
            n_copy(j, i).start()
            return carry

        lax.fori_loop(0, n_y - 1, body, 0)

        @pl.when(core != side)
        def _():
            n_copy(j, n_y - 1).start()

        @pl.when(core == side)
        def _():
            n_all[j, lax.rem(ri, half)] = nt[pl.ds(pl.multiple_of(j * tile + y * wider, wider), wider)]

    def n_drain(j):
        def body(i, carry):
            n_copy(j, i).wait_send()
            return carry

        lax.fori_loop(0, n_y - 1, body, 0)

        @pl.when(core != side)
        def _():
            n_copy(j, n_y - 1).wait_send()

    def n_arrive(j, s):
        source = core * half + s

        @pl.when(source != ri)
        def _():
            remote(
                nt.at[pl.ds(0, wider)], n_all.at[j, s], n_ss.at[j, 0], n_rs.at[j, s], {"ri": source}
            ).wait_recv()

    spread_b(0)
    for j in (1, 2):
        b_in[j].wait()
        widen_b(j)
        regroup(wide, tile, bt, j * tile)
        spread_b(j)

    to_right.wait_recv()
    to_left.wait_recv()
    for i, (band, shift) in enumerate(((occ_left, 0), (occ_own, 0), (occ_right, -1))):
        flag = tm_ref[0, i].astype(F32)
        for j in range(5):
            k = j + shift
            if 0 <= k < band.shape[1] // tile:
                block = band[:, pl.ds(k * tile, tile)].astype(F32) * flag
                green[pl.ds(j * tile, tile), pl.ds(i * tile, tile)] = block.T.astype(BF16)
            else:
                green[pl.ds(j * tile, tile), pl.ds(i * tile, tile)] = jnp.zeros((tile, tile), BF16)

    def make_m(first, count):
        lhs_rows = pl.ds(first * tile, count * tile)

        def body(q, carry):
            pair = jnp.concatenate([b_ref[2 * q], b_ref[2 * q + 1]], axis=1)
            got = jnp.dot(green[lhs_rows, :], pair, preferred_element_type=F32).astype(BF16)
            m_buf[2 * q, lhs_rows, :] = got[:, :tile]
            m_buf[2 * q + 1, lhs_rows, :] = got[:, tile:]
            return carry

        lax.fori_loop(0, rows // 2, body, 0)

    def m_copies(j):
        cols = pl.ds(j * tile, tile)
        return (
            remote(m_buf.at[:, pl.ds((j + 2) * tile, tile), :], m_left.at[:, cols, :], m_ss.at[0, j], m_rs.at[0, j], {"ao": right}),
            remote(m_buf.at[:, cols, :], m_right.at[:, cols, :], m_ss.at[1, j], m_rs.at[1, j], {"ao": left}),
        )

    make_m(0, 3)
    for copy in m_copies(0):
        copy.start()
    make_m(3, 1)
    for copy in m_copies(1):
        copy.start()
    make_m(4, 1)
    for copy in m_copies(2):
        copy.start()

    for j in range(3):
        for copy in m_copies(j):
            copy.wait_recv()

        def n_body(p, carry, j=j):
            needed = jnp.concatenate(
                [
                    m_left[p, pl.ds(j * tile, tile), :],
                    m_buf[p, pl.ds((j + 1) * tile, tile), :],
                    m_right[p, pl.ds(j * tile, tile), :],
                ],
                axis=1,
            )
            wide[pl.ds(pl.multiple_of(p * tile, tile), tile), :] = lax.dot_general(
                needed, virt[...], (((1,), (1,)), ((), ())), preferred_element_type=F32
            )
            return carry

        lax.fori_loop(0, rows, n_body, 0)
        regroup(wide, tile, nt, j * tile)
        spread_n(j)
        b_arrive(j)
        forward(j).start()

    def chi_part(j, first, count):
        size = count * rows
        total = None
        for l in range(0, wider, 2):
            which, at = l // share, l % share
            lhs = jnp.concatenate(
                [n_all[j, pl.ds(first, count), l + k].reshape(size, tile) for k in (0, 1)], axis=1
            )
            rhs = jnp.concatenate(
                [b_all[j, which, :, at + k].reshape(n_ri * rows, tile) for k in (0, 1)], axis=1
            )
            part = lax.dot_general(lhs, rhs, (((1,), (1,)), ((), ())), preferred_element_type=F32)
            total = part if total is None else total + part
        return total

    for j in range(2):
        forwarded(j).wait_recv()

        def n_wait(s, carry, j=j):
            n_arrive(j, s)
            return carry

        lax.fori_loop(0, half, n_wait, 0)
        acc[...] = chi_part(j, 0, half) if j == 0 else acc[...] + chi_part(j, 0, half)
    forwarded(2).wait_recv()
    to_right.wait_send()
    to_left.wait_send()
    for j in range(3):
        for copy in m_copies(j):
            copy.wait_send()
        b_drain(j)
        forward(j).wait_send()

    def panel_copy(s):
        return remote(
            acc.at[pl.ds(pl.multiple_of(s * rows, rows), rows)],
            panels.at[y],
            p_ss.at[s],
            p_rs.at[y],
            {"ri": core * half + s},
        )

    def last(i, carry):
        chip = lax.rem(y + far_first(i), n_y)

        @pl.when(chip // (n_y // 2) == core)
        def _():
            s0 = 2 * lax.rem(chip, n_y // 2)
            n_arrive(2, s0)
            n_arrive(2, s0 + 1)
            at = pl.ds(pl.multiple_of(s0 * rows, 2 * rows), 2 * rows)
            acc[at, :] = acc[at, :] + chi_part(2, s0, 2)
            for s in (s0, s0 + 1):

                @pl.when(core * half + s != ri)
                def _(s=s):
                    panel_copy(s).start()

        return carry

    lax.fori_loop(0, n_y, last, 0)

    @pl.when(core == side)
    def _():
        panels[y] = acc[pl.ds(pl.multiple_of(lax.rem(ri, half) * rows, rows), rows), :]

    for j in range(3):
        n_drain(j)
    def take_panel(chip, carry):
        source = chip * 2 + side

        @pl.when(source != ri)
        def _():
            remote(acc.at[pl.ds(0, rows)], panels.at[chip], p_ss.at[0], p_rs.at[chip], {"ri": source}).wait_recv()

        return carry

    lax.fori_loop(0, n_y, take_panel, 0)
    own_x[x] = jnp.sum(panels[...], axis=0)
    x_copies = [remote(own_x.at[x], own_x.at[x], x_ss.at[d], x_rs.at[d], {"ao": x_peer(d)}) for d in range(1, n_x)]
    for copy in x_copies:
        copy.start()
    for copy in x_copies:
        copy.wait_recv()
    own_z[z] = jnp.sum(own_x[...], axis=0)
    z_copies = [remote(own_z.at[z], own_z.at[z], z_ss.at[d], z_rs.at[d], {"ao": z_peer(d)}) for d in range(1, n_z)]
    for copy in z_copies:
        copy.start()
    for copy in z_copies:
        copy.wait_recv()
    o_ref[...] = -jnp.sum(own_z[...], axis=0)

    def sent_panel(s, carry):
        @pl.when(core * half + s != ri)
        def _():
            panel_copy(s).wait_send()

        return carry

    lax.fori_loop(0, half, sent_panel, 0)
    for copy in x_copies + z_copies:
        copy.wait_send()


def solution(mesh):
    n_ao, n_ri = mesh.shape["ao"], mesh.shape["ri"]
    n_z = 8
    n_x = n_ao // n_z

    def per_device(three_center, occ_band, virt_band, three_mask, occ_mask, virt_mask):
        rows = three_center.shape[0]
        tile = occ_band.shape[0]
        share = tile // n_ri
        size = n_ri * rows
        dma = pltpu.SemaphoreType.DMA
        vmem = pl.BlockSpec(memory_space=pltpu.VMEM)
        return pl.pallas_call(
            functools.partial(kernel, n_ao, n_ri, n_x, n_z, tile, rows),
            out_shape=jax.ShapeDtypeStruct((rows, size), F32),
            in_specs=[pl.BlockSpec(memory_space=pl.ANY)] * 6,
            out_specs=vmem,
            scratch_shapes=[
                pltpu.VMEM((rows, 3 * tile, tile), BF16),
                pltpu.VMEM((tile, 5 * tile), BF16),
                pltpu.VMEM((tile, 3 * tile), BF16),
                pltpu.SMEM((1, 3), jnp.int32),
                pltpu.SMEM((1, 5), jnp.int32),
                pltpu.SMEM((1, 3), jnp.int32),
                pltpu.VMEM((rows * tile, tile), F32),
                pltpu.VMEM((3 * tile, rows, tile), BF16),
                pltpu.VMEM((tile, 5 * tile), BF16),
                pltpu.VMEM((tile, 4 * tile), BF16),
                pltpu.VMEM((tile, 4 * tile), BF16),
                pltpu.VMEM((5 * tile, 3 * tile), BF16),
                pltpu.VMEM((tile, 3 * tile), BF16),
                pltpu.VMEM((rows, 5 * tile, tile), BF16),
                pltpu.VMEM((rows, 3 * tile, tile), BF16),
                pltpu.VMEM((rows, 3 * tile, tile), BF16),
                pltpu.VMEM((3 * tile, rows, tile), BF16),
                pltpu.VMEM((3, 2, n_ri, share, rows, tile), BF16),
                pltpu.VMEM((3, n_ri // 2, 2 * share, rows, tile), BF16),
                pltpu.VMEM((size // 2, size), F32),
                pltpu.VMEM((n_ri // 2, rows, size), F32),
                pltpu.VMEM((n_x, rows, size), F32),
                pltpu.VMEM((n_z, rows, size), F32),
                dma((8,)),
                dma((2,)), dma((2,)),
                dma((2, 3)), dma((2, 3)),
                dma((3, n_ri)), dma((3, n_ri)),
                dma((3,)), dma((3,)),
                dma((3, n_ri // 2)), dma((3, n_ri // 2)),
                dma((n_ri // 2,)), dma((n_ri // 2,)),
                dma((n_x,)), dma((n_x,)),
                dma((n_z,)), dma((n_z,)),
            ],
            compiler_params=pltpu.CompilerParams(collective_id=0, has_side_effects=True),
        )(three_center, occ_band, virt_band, three_mask, occ_mask, virt_mask)

    return jax.shard_map(
        per_device,
        mesh=mesh,
        in_specs=(P("ri", "ao", None), P("ao", None), P("ao", None), P("ao", None), P("ao", None), P("ao", None)),
        out_specs=P("ri", None),
        check_vma=False,
    )
```

```python
import functools

import jax
import jax.numpy as jnp
from jax import lax
from jax.experimental import pallas as pl
from jax.experimental.pallas import tpu as pltpu
from jax.sharding import PartitionSpec as P

MESH = pl.DeviceIdType.MESH
F32 = jnp.float32
BF16 = jnp.bfloat16


def kernel(
    n_ao, n_ri, n_x, n_z, tile, rows,
    b_hbm, occ_hbm, virt_hbm, tm_hbm, om_hbm, vm_hbm, o_ref,
    b_ref, occ_ref, virt_ref, tm_ref, om_ref, vm_ref,
    wide, bt, occ_own, occ_left, occ_right, green, virt, m_buf, m_left, m_right,
    nt, b_all, n_all, acc, panels, own_x, own_z,
    in_sem, occ_ss, occ_rs, m_ss, m_rs, b_ss, b_rs, f_ss, f_rs, n_ss, n_rs, p_ss, p_rs, x_ss, x_rs, z_ss, z_rs,
):
    ao = lax.axis_index("ao")
    ri = lax.axis_index("ri")
    x, z = ao // n_z, lax.rem(ao, n_z)
    y, core = ri // 2, lax.rem(ri, 2)
    n_y = n_ri // 2
    half = n_ri // 2
    side = ri // half
    right, left = lax.rem(ao + 1, n_ao), lax.rem(ao + n_ao - 1, n_ao)
    share = tile // n_ri
    wider = 2 * share

    def far_first(i):
        step = (i + 1) // 2
        return n_y // 2 + step - 2 * step * lax.rem(i, 2)

    def remote(src, dst, ss, rs, where):
        return pltpu.make_async_remote_copy(
            src_ref=src, dst_ref=dst, send_sem=ss, recv_sem=rs, device_id=where, device_id_type=MESH
        )

    def ri_peer(d):
        return lax.rem(ri + d, n_ri)

    def x_peer(d):
        return lax.rem(x + d, n_x) * n_z + z

    def z_peer(d):
        return x * n_z + lax.rem(z + d, n_z)

    b_in = [
        pltpu.make_async_copy(
            b_hbm.at[:, pl.ds(j * tile, tile), :], b_ref.at[:, pl.ds(j * tile, tile), :], in_sem.at[j]
        )
        for j in range(3)
    ]
    small_in = [
        pltpu.make_async_copy(source, target, in_sem.at[3 + i])
        for i, (source, target) in enumerate(
            ((tm_hbm, tm_ref), (om_hbm, om_ref), (vm_hbm, vm_ref), (occ_hbm, occ_ref), (virt_hbm, virt_ref))
        )
    ]
    b_in[0].start()
    for copy in small_in:
        copy.start()
    b_in[1].start()
    b_in[2].start()

    barrier = pltpu.get_barrier_semaphore()

    def greet(where):
        pl.semaphore_signal(barrier, inc=1, device_id=where, device_id_type=MESH)

    def greet_ri(i, carry):
        greet({"ri": lax.rem(y + far_first(i // 2), n_y) * 2 + lax.rem(core + 1 + i, 2)})
        return carry

    lax.fori_loop(0, n_ri - 1, greet_ri, 0)
    greet({"ao": right})
    greet({"ao": left})
    for d in range(1, n_z):
        greet({"ao": z_peer(d)})
    for d in range(1, n_x):
        greet({"ao": x_peer(d)})

    for copy in small_in:
        copy.wait()
    for j in range(5):
        cols = pl.ds(j * tile, tile)
        occ_own[:, cols] = (occ_ref[:, cols].astype(F32) * om_ref[0, j].astype(F32)).astype(BF16)
    for j in range(3):
        cols = pl.ds(j * tile, tile)
        virt[:, cols] = (virt_ref[:, cols].astype(F32) * vm_ref[0, j].astype(F32)).astype(BF16)

    def regroup(source_rows, stride, target, lam0):
        def body(l, carry):
            target[lam0 + l] = source_rows[pl.ds(l, rows, stride=stride), :].astype(BF16)
            return carry

        lax.fori_loop(0, tile, body, 0, unroll=8)

    def widen_b(j):
        flag = tm_ref[0, j].astype(F32)

        def body(p, carry):
            wide[pl.ds(pl.multiple_of(p * tile, tile), tile), :] = (
                b_ref[p, pl.ds(j * tile, tile), :].astype(F32) * flag
            )
            return carry

        lax.fori_loop(0, rows, body, 0)

    b_in[0].wait()
    widen_b(0)
    regroup(wide, tile, bt, 0)

    pl.semaphore_wait(barrier, 2 + n_ri - 1 + n_z - 1 + n_x - 1)

    to_right = remote(occ_own.at[:, pl.ds(tile, 4 * tile)], occ_left, occ_ss.at[0], occ_rs.at[0], {"ao": right})
    to_left = remote(occ_own.at[:, pl.ds(0, 4 * tile)], occ_right, occ_ss.at[1], occ_rs.at[1], {"ao": left})
    to_right.start()
    to_left.start()

    def b_copy(j, i):
        peer = lax.rem(y + far_first(i // 2), n_y) * 2 + lax.rem(core + 1 + i, 2)
        return remote(
            bt.at[pl.ds(pl.multiple_of(j * tile + peer * share, share), share)],
            b_all.at[j, core_of(peer), ri],
            b_ss.at[j],
            b_rs.at[j],
            {"ri": peer},
        )

    def core_of(peer):
        return lax.rem(peer, 2)

    def spread_b(j):
        def body(i, carry):
            b_copy(j, i).start()
            return carry

        lax.fori_loop(0, n_ri - 1, body, 0)
        b_all[j, core, ri] = bt[pl.ds(pl.multiple_of(j * tile + ri * share, share), share)]

    def b_all_of(j):
        rest = bt.at[pl.ds(0, (n_ri - 1) * share)]
        return remote(rest, rest, b_ss.at[j], b_rs.at[j], {"ri": y * 2 + 1 - core})

    def forward(j):
        return remote(b_all.at[j, core], b_all.at[j, core], f_ss.at[j], f_rs.at[j], {"ri": y * 2 + 1 - core})

    def forwarded(j):
        return remote(b_all.at[j, 1 - core], b_all.at[j, 1 - core], f_ss.at[j], f_rs.at[j], {"ri": y * 2 + 1 - core})

    def n_copy(j, i):
        chip = lax.rem(y + far_first(i), n_y)
        return remote(
            nt.at[pl.ds(pl.multiple_of(j * tile + chip * wider, wider), wider)],
            n_all.at[j, lax.rem(ri, half)],
            n_ss.at[j],
            n_rs.at[j if j < 2 else 2 + lax.rem(ri, half) // 2],
            {"ri": chip * 2 + side},
        )

    def spread_n(j):
        def body(i, carry):
            n_copy(j, i).start()
            return carry

        lax.fori_loop(0, n_y - 1, body, 0)

        @pl.when(core != side)
        def _():
            n_copy(j, n_y - 1).start()

        @pl.when(core == side)
        def _():
            n_all[j, lax.rem(ri, half)] = nt[pl.ds(pl.multiple_of(j * tile + y * wider, wider), wider)]

    def n_of(sources, sem, ss):
        some = nt.at[pl.ds(0, sources * wider)]
        return remote(some, some, ss, n_rs.at[sem], {"ri": y * 2 + 1 - core})

    def n_drain(j):
        @pl.when(core != side)
        def _():
            n_of(n_y, 0, n_ss.at[j]).wait_send()

        @pl.when(core == side)
        def _():
            n_of(n_y - 1, 0, n_ss.at[j]).wait_send()

    def n_arrive(j):
        @pl.when(core != side)
        def _():
            n_of(half, j, n_ss.at[j]).wait_recv()

        @pl.when(core == side)
        def _():
            n_of(half - 1, j, n_ss.at[j]).wait_recv()

    spread_b(0)
    for j in (1, 2):
        b_in[j].wait()
        widen_b(j)
        regroup(wide, tile, bt, j * tile)
        spread_b(j)

    to_right.wait_recv()
    to_left.wait_recv()
    for i, (band, shift) in enumerate(((occ_left, 0), (occ_own, 0), (occ_right, -1))):
        flag = tm_ref[0, i].astype(F32)
        for j in range(5):
            k = j + shift
            if 0 <= k < band.shape[1] // tile:
                block = band[:, pl.ds(k * tile, tile)].astype(F32) * flag
                green[pl.ds(j * tile, tile), pl.ds(i * tile, tile)] = block.T.astype(BF16)
            else:
                green[pl.ds(j * tile, tile), pl.ds(i * tile, tile)] = jnp.zeros((tile, tile), BF16)

    def make_m(first, count):
        lhs_rows = pl.ds(first * tile, count * tile)

        def body(q, carry):
            pair = jnp.concatenate([b_ref[2 * q], b_ref[2 * q + 1]], axis=1)
            got = jnp.dot(green[lhs_rows, :], pair, preferred_element_type=F32).astype(BF16)
            m_buf[2 * q, lhs_rows, :] = got[:, :tile]
            m_buf[2 * q + 1, lhs_rows, :] = got[:, tile:]
            return carry

        lax.fori_loop(0, rows // 2, body, 0)

    def m_copies(j):
        cols = pl.ds(j * tile, tile)
        return (
            remote(m_buf.at[:, pl.ds((j + 2) * tile, tile), :], m_left.at[:, cols, :], m_ss.at[j], m_rs.at[j], {"ao": right}),
            remote(m_buf.at[:, cols, :], m_right.at[:, cols, :], m_ss.at[j], m_rs.at[j], {"ao": left}),
        )

    def m_both(j):
        both = m_left.at[:, pl.ds(0, 2 * tile), :]
        return remote(both, both, m_ss.at[j], m_rs.at[j], {"ao": right})

    make_m(0, 3)
    for copy in m_copies(0):
        copy.start()
    make_m(3, 1)
    for copy in m_copies(1):
        copy.start()
    make_m(4, 1)
    for copy in m_copies(2):
        copy.start()

    for j in range(3):
        m_both(j).wait_recv()

        def n_body(p, carry, j=j):
            needed = jnp.concatenate(
                [
                    m_left[p, pl.ds(j * tile, tile), :],
                    m_buf[p, pl.ds((j + 1) * tile, tile), :],
                    m_right[p, pl.ds(j * tile, tile), :],
                ],
                axis=1,
            )
            wide[pl.ds(pl.multiple_of(p * tile, tile), tile), :] = lax.dot_general(
                needed, virt[...], (((1,), (1,)), ((), ())), preferred_element_type=F32
            )
            return carry

        lax.fori_loop(0, rows, n_body, 0)
        regroup(wide, tile, nt, j * tile)
        spread_n(j)
        b_all_of(j).wait_recv()
        forward(j).start()

    def chi_part(j, first, count):
        size = count * rows
        total = None
        for l in range(0, wider, 2):
            which, at = l // share, l % share
            lhs = jnp.concatenate(
                [n_all[j, pl.ds(first, count), l + k].reshape(size, tile) for k in (0, 1)], axis=1
            )
            rhs = jnp.concatenate(
                [b_all[j, which, :, at + k].reshape(n_ri * rows, tile) for k in (0, 1)], axis=1
            )
            part = lax.dot_general(lhs, rhs, (((1,), (1,)), ((), ())), preferred_element_type=F32)
            total = part if total is None else total + part
        return total

    for j in range(2):
        forwarded(j).wait_recv()

        n_arrive(j)
        acc[...] = chi_part(j, 0, half) if j == 0 else acc[...] + chi_part(j, 0, half)
    forwarded(2).wait_recv()
    to_right.wait_send()
    to_left.wait_send()
    for j in range(3):
        m_both(j).wait_send()
        b_all_of(j).wait_send()
        forward(j).wait_send()

    def panel_copy(s):
        return remote(
            acc.at[pl.ds(pl.multiple_of(s * rows, rows), rows)],
            panels.at[y],
            p_ss,
            p_rs,
            {"ri": core * half + s},
        )

    def last(i, carry):
        chip = lax.rem(y + far_first(i), n_y)

        @pl.when(chip // (n_y // 2) == core)
        def _():
            s0 = 2 * lax.rem(chip, n_y // 2)

            @pl.when(chip != y)
            def _():
                n_of(2, 2 + s0 // 2, n_ss.at[2]).wait_recv()

            @pl.when(chip == y)
            def _():
                n_of(1, 2 + s0 // 2, n_ss.at[2]).wait_recv()

            at = pl.ds(pl.multiple_of(s0 * rows, 2 * rows), 2 * rows)
            acc[at, :] = acc[at, :] + chi_part(2, s0, 2)
            for s in (s0, s0 + 1):

                @pl.when(core * half + s != ri)
                def _(s=s):
                    panel_copy(s).start()

        return carry

    lax.fori_loop(0, n_y, last, 0)

    @pl.when(core == side)
    def _():
        panels[y] = acc[pl.ds(pl.multiple_of(lax.rem(ri, half) * rows, rows), rows), :]

    for j in range(3):
        n_drain(j)
    def panels_of(count):
        some = acc.at[pl.ds(0, count * rows)]
        return remote(some, some, p_ss, p_rs, {"ri": y * 2 + 1 - core})

    @pl.when(core != side)
    def _():
        panels_of(n_y).wait_recv()

    @pl.when(core == side)
    def _():
        panels_of(n_y - 1).wait_recv()

    own_x[x] = jnp.sum(panels[...], axis=0)
    for d in range(1, n_x):
        remote(own_x.at[x], own_x.at[x], x_ss, x_rs, {"ao": x_peer(d)}).start()

    def rest_of(ref, count, ss, rs, where):
        return remote(ref.at[pl.ds(0, count)], ref.at[pl.ds(0, count)], ss, rs, where)

    if n_x > 1:
        x_rest = rest_of(own_x, n_x - 1, x_ss, x_rs, {"ao": x_peer(1)})
        x_rest.wait_recv()
    own_z[z] = jnp.sum(own_x[...], axis=0)
    for d in range(1, n_z):
        remote(own_z.at[z], own_z.at[z], z_ss, z_rs, {"ao": z_peer(d)}).start()
    z_rest = rest_of(own_z, n_z - 1, z_ss, z_rs, {"ao": z_peer(1)})
    z_rest.wait_recv()
    o_ref[...] = -jnp.sum(own_z[...], axis=0)

    @pl.when(core != side)
    def _():
        panels_of(half).wait_send()

    @pl.when(core == side)
    def _():
        panels_of(half - 1).wait_send()

    if n_x > 1:
        x_rest.wait_send()
    z_rest.wait_send()


def solution(mesh):
    n_ao, n_ri = mesh.shape["ao"], mesh.shape["ri"]
    n_z = 8
    n_x = n_ao // n_z

    def per_device(three_center, occ_band, virt_band, three_mask, occ_mask, virt_mask):
        rows = three_center.shape[0]
        tile = occ_band.shape[0]
        share = tile // n_ri
        size = n_ri * rows
        dma = pltpu.SemaphoreType.DMA
        vmem = pl.BlockSpec(memory_space=pltpu.VMEM)
        return pl.pallas_call(
            functools.partial(kernel, n_ao, n_ri, n_x, n_z, tile, rows),
            out_shape=pltpu.VMEM((rows, size), F32),
            in_specs=[pl.BlockSpec(memory_space=pl.ANY)] * 6,
            out_specs=vmem,
            scratch_shapes=[
                pltpu.VMEM((rows, 3 * tile, tile), BF16),
                pltpu.VMEM((tile, 5 * tile), BF16),
                pltpu.VMEM((tile, 3 * tile), BF16),
                pltpu.SMEM((1, 3), jnp.int32),
                pltpu.SMEM((1, 5), jnp.int32),
                pltpu.SMEM((1, 3), jnp.int32),
                pltpu.VMEM((rows * tile, tile), F32),
                pltpu.VMEM((3 * tile, rows, tile), BF16),
                pltpu.VMEM((tile, 5 * tile), BF16),
                pltpu.VMEM((tile, 4 * tile), BF16),
                pltpu.VMEM((tile, 4 * tile), BF16),
                pltpu.VMEM((5 * tile, 3 * tile), BF16),
                pltpu.VMEM((tile, 3 * tile), BF16),
                pltpu.VMEM((rows, 5 * tile, tile), BF16),
                pltpu.VMEM((rows, 3 * tile, tile), BF16),
                pltpu.VMEM((rows, 3 * tile, tile), BF16),
                pltpu.VMEM((3 * tile, rows, tile), BF16),
                pltpu.VMEM((3, 2, n_ri, share, rows, tile), BF16),
                pltpu.VMEM((3, n_ri // 2, 2 * share, rows, tile), BF16),
                pltpu.VMEM((size // 2, size), F32),
                pltpu.VMEM((n_ri // 2, rows, size), F32),
                pltpu.VMEM((n_x, rows, size), F32),
                pltpu.VMEM((n_z, rows, size), F32),
                dma((8,)),
                dma((2,)), dma((2,)),
                dma((3,)), dma((3,)),
                dma((3,)), dma((3,)),
                dma((3,)), dma((3,)),
                dma((3,)), dma((2 + n_ri // 4,)),
                dma, dma, dma, dma, dma, dma,
            ],
            compiler_params=pltpu.CompilerParams(collective_id=0, has_side_effects=True),
        )(three_center, occ_band, virt_band, three_mask, occ_mask, virt_mask)

    return jax.shard_map(
        per_device,
        mesh=mesh,
        in_specs=(P("ri", "ao", None), P("ao", None), P("ao", None), P("ao", None), P("ao", None), P("ao", None)),
        out_specs=P("ri", None),
        check_vma=False,
    )
```

```python
import functools

import jax
import jax.numpy as jnp
from jax import lax
from jax.experimental import pallas as pl
from jax.experimental.pallas import tpu as pltpu
from jax.sharding import PartitionSpec as P

MESH = pl.DeviceIdType.MESH
F32 = jnp.float32
BF16 = jnp.bfloat16


def kernel(
    n_ao, n_ri, n_x, n_z, tile, rows,
    b_hbm, occ_hbm, virt_hbm, tm_hbm, om_hbm, vm_hbm, o_ref,
    b_ref, occ_ref, virt_ref, tm_ref, om_ref, vm_ref,
    wide, bt, occ_own, occ_left, occ_right, green, virt, m_buf, m_left, m_right,
    nt, b_all, n_all, acc, done, panels, own_x, own_z,
    in_sem, occ_ss, occ_rs, m_ss, m_rs, b_ss, b_rs, f_ss, f_rs, n_ss, n_rs, p_ss, p_rs, x_ss, x_rs, z_ss, z_rs,
):
    ao = lax.axis_index("ao")
    ri = lax.axis_index("ri")
    x, z = ao // n_z, lax.rem(ao, n_z)
    y, core = ri // 2, lax.rem(ri, 2)
    n_y = n_ri // 2
    half = n_ri // 2
    side = ri // half
    right, left = lax.rem(ao + 1, n_ao), lax.rem(ao + n_ao - 1, n_ao)
    share = tile // n_ri
    wider = 2 * share

    def far_first(i):
        step = (i + 1) // 2
        return n_y // 2 + step - 2 * step * lax.rem(i, 2)

    def remote(src, dst, ss, rs, where):
        return pltpu.make_async_remote_copy(
            src_ref=src, dst_ref=dst, send_sem=ss, recv_sem=rs, device_id=where, device_id_type=MESH
        )

    def ri_peer(d):
        return lax.rem(ri + d, n_ri)

    def x_peer(d):
        return lax.rem(x + d, n_x) * n_z + z

    def z_peer(d):
        return x * n_z + lax.rem(z + d, n_z)

    b_in = [
        pltpu.make_async_copy(
            b_hbm.at[:, pl.ds(j * tile, tile), :], b_ref.at[:, pl.ds(j * tile, tile), :], in_sem.at[j]
        )
        for j in range(3)
    ]
    small_in = [
        pltpu.make_async_copy(source, target, in_sem.at[3 + i])
        for i, (source, target) in enumerate(
            ((tm_hbm, tm_ref), (om_hbm, om_ref), (vm_hbm, vm_ref), (occ_hbm, occ_ref), (virt_hbm, virt_ref))
        )
    ]
    b_in[0].start()
    for copy in small_in:
        copy.start()
    b_in[1].start()
    b_in[2].start()

    barrier = pltpu.get_barrier_semaphore()

    def greet(where):
        pl.semaphore_signal(barrier, inc=1, device_id=where, device_id_type=MESH)

    def greet_ri(i, carry):
        greet({"ri": lax.rem(y + far_first(i // 2), n_y) * 2 + lax.rem(core + 1 + i, 2)})
        return carry

    lax.fori_loop(0, n_ri - 1, greet_ri, 0)
    greet({"ao": right})
    greet({"ao": left})
    for d in range(1, n_z):
        greet({"ao": z_peer(d)})
    for d in range(1, n_x):
        greet({"ao": x_peer(d)})

    def regroup(source_rows, stride, target, lam0):
        def body(l, carry):
            target[lam0 + l] = source_rows[pl.ds(l, rows, stride=stride), :].astype(BF16)
            return carry

        lax.fori_loop(0, tile, body, 0, unroll=8)

    def widen_b(j):
        flag = tm_ref[0, j].astype(F32)

        def body(p, carry):
            wide[pl.ds(pl.multiple_of(p * tile, tile), tile), :] = (
                b_ref[p, pl.ds(j * tile, tile), :].astype(F32) * flag
            )
            return carry

        lax.fori_loop(0, rows, body, 0)

    small_in[0].wait()
    b_in[0].wait()
    widen_b(0)
    regroup(wide, tile, bt, 0)

    pl.semaphore_wait(barrier, 2 + n_ri - 1 + n_z - 1 + n_x - 1)


    def b_copy(j, i):
        peer = lax.rem(y + far_first(i // 2), n_y) * 2 + lax.rem(core + 1 + i, 2)
        return remote(
            bt.at[pl.ds(pl.multiple_of(j * tile + peer * share, share), share)],
            b_all.at[j, core_of(peer), ri],
            b_ss.at[j],
            b_rs.at[j],
            {"ri": peer},
        )

    def core_of(peer):
        return lax.rem(peer, 2)

    def spread_b(j):
        def body(i, carry):
            b_copy(j, i).start()
            return carry

        lax.fori_loop(0, n_ri - 1, body, 0)
        b_all[j, core, ri] = bt[pl.ds(pl.multiple_of(j * tile + ri * share, share), share)]

    def b_all_of(j):
        rest = bt.at[pl.ds(0, (n_ri - 1) * share)]
        return remote(rest, rest, b_ss.at[j], b_rs.at[j], {"ri": y * 2 + 1 - core})

    def forward(j):
        return remote(b_all.at[j, core], b_all.at[j, core], f_ss.at[j], f_rs.at[j], {"ri": y * 2 + 1 - core})

    def forwarded(j):
        return remote(b_all.at[j, 1 - core], b_all.at[j, 1 - core], f_ss.at[j], f_rs.at[j], {"ri": y * 2 + 1 - core})

    def n_copy(j, i):
        chip = lax.rem(y + far_first(i), n_y)
        return remote(
            nt.at[pl.ds(pl.multiple_of(j * tile + chip * wider, wider), wider)],
            n_all.at[j, lax.rem(ri, half)],
            n_ss.at[j],
            n_rs.at[j if j < 2 else 2 + lax.rem(ri, half) // 2],
            {"ri": chip * 2 + side},
        )

    def spread_n(j):
        def body(i, carry):
            n_copy(j, i).start()
            return carry

        lax.fori_loop(0, n_y - 1, body, 0)

        @pl.when(core != side)
        def _():
            n_copy(j, n_y - 1).start()

        @pl.when(core == side)
        def _():
            n_all[j, lax.rem(ri, half)] = nt[pl.ds(pl.multiple_of(j * tile + y * wider, wider), wider)]

    def n_of(sources, sem, ss):
        some = nt.at[pl.ds(0, sources * wider)]
        return remote(some, some, ss, n_rs.at[sem], {"ri": y * 2 + 1 - core})

    def n_drain(j):
        @pl.when(core != side)
        def _():
            n_of(n_y, 0, n_ss.at[j]).wait_send()

        @pl.when(core == side)
        def _():
            n_of(n_y - 1, 0, n_ss.at[j]).wait_send()

    def n_arrive(j):
        @pl.when(core != side)
        def _():
            n_of(half, j, n_ss.at[j]).wait_recv()

        @pl.when(core == side)
        def _():
            n_of(half - 1, j, n_ss.at[j]).wait_recv()

    spread_b(0)
    for copy in small_in[1:]:
        copy.wait()
    for j in range(5):
        cols = pl.ds(j * tile, tile)
        occ_own[:, cols] = (occ_ref[:, cols].astype(F32) * om_ref[0, j].astype(F32)).astype(BF16)
    for j in range(3):
        cols = pl.ds(j * tile, tile)
        virt[:, cols] = (virt_ref[:, cols].astype(F32) * vm_ref[0, j].astype(F32)).astype(BF16)

    to_right = remote(occ_own.at[:, pl.ds(tile, 4 * tile)], occ_left, occ_ss.at[0], occ_rs.at[0], {"ao": right})
    to_left = remote(occ_own.at[:, pl.ds(0, 4 * tile)], occ_right, occ_ss.at[1], occ_rs.at[1], {"ao": left})
    to_right.start()
    to_left.start()

    for j in (1, 2):
        b_in[j].wait()
        widen_b(j)
        regroup(wide, tile, bt, j * tile)
        spread_b(j)

    to_right.wait_recv()
    to_left.wait_recv()
    for i, (band, shift) in enumerate(((occ_left, 0), (occ_own, 0), (occ_right, -1))):
        flag = tm_ref[0, i].astype(F32)
        for j in range(5):
            k = j + shift
            if 0 <= k < band.shape[1] // tile:
                block = band[:, pl.ds(k * tile, tile)].astype(F32) * flag
                green[pl.ds(j * tile, tile), pl.ds(i * tile, tile)] = block.T.astype(BF16)
            else:
                green[pl.ds(j * tile, tile), pl.ds(i * tile, tile)] = jnp.zeros((tile, tile), BF16)

    def make_m(first, count):
        lhs_rows = pl.ds(first * tile, count * tile)

        def body(q, carry):
            pair = jnp.concatenate([b_ref[2 * q], b_ref[2 * q + 1]], axis=1)
            got = jnp.dot(green[lhs_rows, :], pair, preferred_element_type=F32).astype(BF16)
            m_buf[2 * q, lhs_rows, :] = got[:, :tile]
            m_buf[2 * q + 1, lhs_rows, :] = got[:, tile:]
            return carry

        lax.fori_loop(0, rows // 2, body, 0)

    def m_copies(j):
        cols = pl.ds(j * tile, tile)
        return (
            remote(m_buf.at[:, pl.ds((j + 2) * tile, tile), :], m_left.at[:, cols, :], m_ss.at[j], m_rs.at[j], {"ao": right}),
            remote(m_buf.at[:, cols, :], m_right.at[:, cols, :], m_ss.at[j], m_rs.at[j], {"ao": left}),
        )

    def m_both(j):
        both = m_left.at[:, pl.ds(0, 2 * tile), :]
        return remote(both, both, m_ss.at[j], m_rs.at[j], {"ao": right})

    make_m(0, 3)
    for copy in m_copies(0):
        copy.start()
    make_m(3, 1)
    for copy in m_copies(1):
        copy.start()
    make_m(4, 1)
    for copy in m_copies(2):
        copy.start()

    for j in range(3):
        m_both(j).wait_recv()

        def n_body(p, carry, j=j):
            needed = jnp.concatenate(
                [
                    m_left[p, pl.ds(j * tile, tile), :],
                    m_buf[p, pl.ds((j + 1) * tile, tile), :],
                    m_right[p, pl.ds(j * tile, tile), :],
                ],
                axis=1,
            )
            wide[pl.ds(pl.multiple_of(p * tile, tile), tile), :] = lax.dot_general(
                needed, virt[...], (((1,), (1,)), ((), ())), preferred_element_type=F32
            )
            return carry

        lax.fori_loop(0, rows, n_body, 0)
        regroup(wide, tile, nt, j * tile)
        spread_n(j)
        b_all_of(j).wait_recv()
        forward(j).start()

    def chi_part(j, first, count):
        size = count * rows
        total = None
        for l in range(0, wider, 2):
            which, at = l // share, l % share
            lhs = jnp.concatenate(
                [n_all[j, pl.ds(first, count), l + k].reshape(size, tile) for k in (0, 1)], axis=1
            )
            rhs = jnp.concatenate(
                [b_all[j, which, :, at + k].reshape(n_ri * rows, tile) for k in (0, 1)], axis=1
            )
            part = lax.dot_general(lhs, rhs, (((1,), (1,)), ((), ())), preferred_element_type=F32)
            total = part if total is None else total + part
        return total

    for j in range(2):
        forwarded(j).wait_recv()

        n_arrive(j)
        acc[...] = chi_part(j, 0, half) if j == 0 else acc[...] + chi_part(j, 0, half)
    forwarded(2).wait_recv()
    to_right.wait_send()
    to_left.wait_send()
    for j in range(3):
        m_both(j).wait_send()
        b_all_of(j).wait_send()
        forward(j).wait_send()

    def panel_copy(s):
        return remote(
            done.at[pl.ds(pl.multiple_of(s * rows, rows), rows)],
            panels.at[y],
            p_ss,
            p_rs,
            {"ri": core * half + s},
        )

    def last(i, carry):
        chip = lax.rem(y + far_first(i), n_y)

        @pl.when(chip // (n_y // 2) == core)
        def _():
            s0 = 2 * lax.rem(chip, n_y // 2)

            @pl.when(chip != y)
            def _():
                n_of(2, 2 + s0 // 2, n_ss.at[2]).wait_recv()

            @pl.when(chip == y)
            def _():
                n_of(1, 2 + s0 // 2, n_ss.at[2]).wait_recv()

            at = pl.ds(pl.multiple_of(s0 * rows, 2 * rows), 2 * rows)
            done[at, :] = (acc[at, :] + chi_part(2, s0, 2)).astype(BF16)
            for s in (s0, s0 + 1):

                @pl.when(core * half + s != ri)
                def _(s=s):
                    panel_copy(s).start()

        return carry

    lax.fori_loop(0, n_y, last, 0)

    @pl.when(core == side)
    def _():
        panels[y] = done[pl.ds(pl.multiple_of(lax.rem(ri, half) * rows, rows), rows), :]

    for j in range(3):
        n_drain(j)
    def panels_of(count):
        some = done.at[pl.ds(0, count * rows)]
        return remote(some, some, p_ss, p_rs, {"ri": y * 2 + 1 - core})

    @pl.when(core != side)
    def _():
        panels_of(n_y).wait_recv()

    @pl.when(core == side)
    def _():
        panels_of(n_y - 1).wait_recv()

    own_x[x] = jnp.sum(panels[...].astype(F32), axis=0)
    for d in range(1, n_x):
        remote(own_x.at[x], own_x.at[x], x_ss, x_rs, {"ao": x_peer(d)}).start()

    def rest_of(ref, count, ss, rs, where):
        return remote(ref.at[pl.ds(0, count)], ref.at[pl.ds(0, count)], ss, rs, where)

    if n_x > 1:
        x_rest = rest_of(own_x, n_x - 1, x_ss, x_rs, {"ao": x_peer(1)})
        x_rest.wait_recv()
    own_z[z] = jnp.sum(own_x[...], axis=0).astype(BF16)
    for i in range(n_z - 1):
        step = (i + 1) // 2
        far = n_z // 2 + (step if i % 2 == 0 else -step)
        remote(own_z.at[z], own_z.at[z], z_ss, z_rs, {"ao": z_peer(far)}).start()
    z_rest = rest_of(own_z, n_z - 1, z_ss, z_rs, {"ao": z_peer(1)})
    z_rest.wait_recv()
    o_ref[...] = -jnp.sum(own_z[...].astype(F32), axis=0)

    @pl.when(core != side)
    def _():
        panels_of(half).wait_send()

    @pl.when(core == side)
    def _():
        panels_of(half - 1).wait_send()

    if n_x > 1:
        x_rest.wait_send()
    z_rest.wait_send()


def solution(mesh):
    n_ao, n_ri = mesh.shape["ao"], mesh.shape["ri"]
    n_z = 8
    n_x = n_ao // n_z

    def per_device(three_center, occ_band, virt_band, three_mask, occ_mask, virt_mask):
        rows = three_center.shape[0]
        tile = occ_band.shape[0]
        share = tile // n_ri
        size = n_ri * rows
        dma = pltpu.SemaphoreType.DMA
        vmem = pl.BlockSpec(memory_space=pltpu.VMEM)
        return pl.pallas_call(
            functools.partial(kernel, n_ao, n_ri, n_x, n_z, tile, rows),
            out_shape=pltpu.VMEM((rows, size), F32),
            in_specs=[pl.BlockSpec(memory_space=pl.ANY)] * 6,
            out_specs=vmem,
            scratch_shapes=[
                pltpu.VMEM((rows, 3 * tile, tile), BF16),
                pltpu.VMEM((tile, 5 * tile), BF16),
                pltpu.VMEM((tile, 3 * tile), BF16),
                pltpu.SMEM((1, 3), jnp.int32),
                pltpu.SMEM((1, 5), jnp.int32),
                pltpu.SMEM((1, 3), jnp.int32),
                pltpu.VMEM((rows * tile, tile), F32),
                pltpu.VMEM((3 * tile, rows, tile), BF16),
                pltpu.VMEM((tile, 5 * tile), BF16),
                pltpu.VMEM((tile, 4 * tile), BF16),
                pltpu.VMEM((tile, 4 * tile), BF16),
                pltpu.VMEM((5 * tile, 3 * tile), BF16),
                pltpu.VMEM((tile, 3 * tile), BF16),
                pltpu.VMEM((rows, 5 * tile, tile), BF16),
                pltpu.VMEM((rows, 3 * tile, tile), BF16),
                pltpu.VMEM((rows, 3 * tile, tile), BF16),
                pltpu.VMEM((3 * tile, rows, tile), BF16),
                pltpu.VMEM((3, 2, n_ri, share, rows, tile), BF16),
                pltpu.VMEM((3, n_ri // 2, 2 * share, rows, tile), BF16),
                pltpu.VMEM((size // 2, size), F32),
                pltpu.VMEM((size // 2, size), BF16),
                pltpu.VMEM((n_ri // 2, rows, size), BF16),
                pltpu.VMEM((n_x, rows, size), F32),
                pltpu.VMEM((n_z, rows, size), BF16),
                dma((8,)),
                dma((2,)), dma((2,)),
                dma((3,)), dma((3,)),
                dma((3,)), dma((3,)),
                dma((3,)), dma((3,)),
                dma((3,)), dma((2 + n_ri // 4,)),
                dma, dma, dma, dma, dma, dma,
            ],
            compiler_params=pltpu.CompilerParams(collective_id=0, has_side_effects=True),
        )(three_center, occ_band, virt_band, three_mask, occ_mask, virt_mask)

    return jax.shard_map(
        per_device,
        mesh=mesh,
        in_specs=(P("ri", "ao", None), P("ao", None), P("ao", None), P("ao", None), P("ao", None), P("ao", None)),
        out_specs=P("ri", None),
        check_vma=False,
    )
```

```python
import functools

import jax
import jax.numpy as jnp
from jax import lax
from jax.experimental import pallas as pl
from jax.experimental.pallas import tpu as pltpu
from jax.sharding import PartitionSpec as P

MESH = pl.DeviceIdType.MESH
F32 = jnp.float32
BF16 = jnp.bfloat16


def kernel(
    n_ao, n_ri, n_x, n_z, tile, rows,
    b_hbm, occ_hbm, virt_hbm, tm_hbm, om_hbm, vm_hbm, o_ref,
    b_ref, occ_ref, virt_ref, tm_ref, om_ref, vm_ref,
    wide, bt, occ_own, occ_left, occ_right, green, virt, m_buf, m_left, m_right,
    nt, b_all, n_all, acc, done, panels, own_x, own_z,
    in_sem, up, down, z_up, z_down, x_up, occ_ss, occ_rs, m_ss, m_rs, b_ss, b_rs, f_ss, f_rs, n_ss, n_rs, p_ss, p_rs, x_ss, x_rs, z_ss, z_rs,
):
    ao = lax.axis_index("ao")
    ri = lax.axis_index("ri")
    x, z = ao // n_z, lax.rem(ao, n_z)
    y, core = ri // 2, lax.rem(ri, 2)
    n_y = n_ri // 2
    half = n_ri // 2
    side = ri // half
    right, left = lax.rem(ao + 1, n_ao), lax.rem(ao + n_ao - 1, n_ao)
    share = tile // n_ri
    wider = 2 * share

    def far_first(i):
        step = (i + 1) // 2
        return n_y // 2 + step - 2 * step * lax.rem(i, 2)

    def remote(src, dst, ss, rs, where):
        return pltpu.make_async_remote_copy(
            src_ref=src, dst_ref=dst, send_sem=ss, recv_sem=rs, device_id=where, device_id_type=MESH
        )

    def ri_peer(d):
        return lax.rem(ri + d, n_ri)

    def x_peer(d):
        return lax.rem(x + d, n_x) * n_z + z

    def z_peer(d):
        return x * n_z + lax.rem(z + d, n_z)

    b_in = [
        pltpu.make_async_copy(
            b_hbm.at[:, pl.ds(j * tile, tile), :], b_ref.at[:, pl.ds(j * tile, tile), :], in_sem.at[j]
        )
        for j in range(3)
    ]
    small_in = [
        pltpu.make_async_copy(source, target, in_sem.at[3 + i])
        for i, (source, target) in enumerate(
            ((tm_hbm, tm_ref), (om_hbm, om_ref), (vm_hbm, vm_ref), (occ_hbm, occ_ref), (virt_hbm, virt_ref))
        )
    ]
    b_in[0].start()
    for copy in small_in:
        copy.start()
    b_in[1].start()
    b_in[2].start()

    barrier = pltpu.get_barrier_semaphore()

    def greet(where):
        pl.semaphore_signal(barrier, inc=1, device_id=where, device_id_type=MESH)

    above, below = lax.rem(y + 1, n_y), lax.rem(y + n_y - 1, n_y)
    for chip in (above, below):
        greet({"ri": chip * 2 + core})
        greet({"ri": chip * 2 + 1 - core})
    greet({"ri": y * 2 + 1 - core})
    x_beside = (1, n_x - 1) if n_x > 1 else ()
    for where in [right, left, z_peer(1), z_peer(n_z - 1)] + [x_peer(d) for d in x_beside]:
        greet({"ao": where})

    def regroup(source_rows, stride, target, lam0):
        def body(l, carry):
            target[lam0 + l] = source_rows[pl.ds(l, rows, stride=stride), :].astype(BF16)
            return carry

        lax.fori_loop(0, tile, body, 0, unroll=8)

    def widen_b(j):
        flag = tm_ref[0, j].astype(F32)

        def body(p, carry):
            wide[pl.ds(pl.multiple_of(p * tile, tile), tile), :] = (
                b_ref[p, pl.ds(j * tile, tile), :].astype(F32) * flag
            )
            return carry

        lax.fori_loop(0, rows, body, 0)

    small_in[0].wait()
    b_in[0].wait()
    widen_b(0)
    regroup(wide, tile, bt, 0)

    pl.semaphore_wait(barrier, 5 + 4 + len(x_beside))

    def tell(step):
        pl.semaphore_signal(up.at[step], inc=1, device_id={"ri": above * 2 + core}, device_id_type=MESH)
        if step < 2:
            pl.semaphore_signal(down.at[step], inc=1, device_id={"ri": below * 2 + core}, device_id_type=MESH)

    def hear(step):
        pl.semaphore_wait(up.at[step], 1)
        if step < 2:
            pl.semaphore_wait(down.at[step], 1)

    def tell_ao(step):
        pl.semaphore_signal(z_up.at[step], inc=1, device_id={"ao": z_peer(1)}, device_id_type=MESH)
        if step < 2:
            pl.semaphore_signal(z_down.at[step], inc=1, device_id={"ao": z_peer(n_z - 1)}, device_id_type=MESH)
        if step == 0 and x_beside:
            pl.semaphore_signal(x_up, inc=1, device_id={"ao": x_peer(1)}, device_id_type=MESH)

    def hear_ao(step):
        pl.semaphore_wait(z_up.at[step], 1)
        if step < 2:
            pl.semaphore_wait(z_down.at[step], 1)
        if step == 0 and x_beside:
            pl.semaphore_wait(x_up, 1)

    tell(0)
    tell_ao(0)


    def b_copy(j, i):
        peer = lax.rem(y + far_first(i // 2), n_y) * 2 + lax.rem(core + 1 + i, 2)
        return remote(
            bt.at[pl.ds(pl.multiple_of(j * tile + peer * share, share), share)],
            b_all.at[j, core_of(peer), ri],
            b_ss.at[j],
            b_rs.at[j],
            {"ri": peer},
        )

    def core_of(peer):
        return lax.rem(peer, 2)

    def spread_b(j):
        def body(i, carry):
            b_copy(j, i).start()
            return carry

        lax.fori_loop(0, n_ri - 2, body, 0)
        own_b(j)

    def own_b(j):
        b_copy(j, n_ri - 2).start()
        b_all[j, core, ri] = bt[pl.ds(pl.multiple_of(j * tile + ri * share, share), share)]

    def b_all_of(j):
        rest = bt.at[pl.ds(0, (n_ri - 1) * share)]
        return remote(rest, rest, b_ss.at[j], b_rs.at[j], {"ri": y * 2 + 1 - core})

    def forward(j):
        return remote(b_all.at[j, core], b_all.at[j, core], f_ss.at[j], f_rs.at[j], {"ri": y * 2 + 1 - core})

    def forwarded(j):
        return remote(b_all.at[j, 1 - core], b_all.at[j, 1 - core], f_ss.at[j], f_rs.at[j], {"ri": y * 2 + 1 - core})

    def n_copy(j, i):
        chip = lax.rem(y + far_first(i), n_y)
        return remote(
            nt.at[pl.ds(pl.multiple_of(j * tile + chip * wider, wider), wider)],
            n_all.at[j, lax.rem(ri, half)],
            n_ss.at[j],
            n_rs.at[j if j < 2 else 2 + lax.rem(ri, half) // 2],
            {"ri": chip * 2 + side},
        )

    def spread_n(j):
        def body(i, carry):
            n_copy(j, i).start()
            return carry

        lax.fori_loop(0, n_y - 1, body, 0)

        @pl.when(core != side)
        def _():
            n_copy(j, n_y - 1).start()

        @pl.when(core == side)
        def _():
            n_all[j, lax.rem(ri, half)] = nt[pl.ds(pl.multiple_of(j * tile + y * wider, wider), wider)]

    def n_of(sources, sem, ss):
        some = nt.at[pl.ds(0, sources * wider)]
        return remote(some, some, ss, n_rs.at[sem], {"ri": y * 2 + 1 - core})

    def n_drain(j):
        @pl.when(core != side)
        def _():
            n_of(n_y, 0, n_ss.at[j]).wait_send()

        @pl.when(core == side)
        def _():
            n_of(n_y - 1, 0, n_ss.at[j]).wait_send()

    def n_arrive(j):
        @pl.when(core != side)
        def _():
            n_of(half, j, n_ss.at[j]).wait_recv()

        @pl.when(core == side)
        def _():
            n_of(half - 1, j, n_ss.at[j]).wait_recv()

    def b_by(j, steps):
        chip = lax.rem(y + steps + n_y, n_y)
        for other in (0, 1):
            peer = chip * 2 + (core if other == 0 else 1 - core)
            remote(
                bt.at[pl.ds(pl.multiple_of(j * tile + peer * share, share), share)],
                b_all.at[j, core_of(peer), ri],
                b_ss.at[j],
                b_rs.at[j],
                {"ri": peer},
            ).start()

    b_by(0, 1)
    b_by(0, -1)
    hear(0)
    tell(1)
    b_by(0, 2)
    b_by(0, -2)
    hear(1)
    tell(2)
    b_by(0, 3)
    b_by(0, -3)
    hear(2)
    b_by(0, 4)
    own_b(0)
    for copy in small_in[1:]:
        copy.wait()
    for j in range(5):
        cols = pl.ds(j * tile, tile)
        occ_own[:, cols] = (occ_ref[:, cols].astype(F32) * om_ref[0, j].astype(F32)).astype(BF16)
    for j in range(3):
        cols = pl.ds(j * tile, tile)
        virt[:, cols] = (virt_ref[:, cols].astype(F32) * vm_ref[0, j].astype(F32)).astype(BF16)

    to_right = remote(occ_own.at[:, pl.ds(tile, 4 * tile)], occ_left, occ_ss.at[0], occ_rs.at[0], {"ao": right})
    to_left = remote(occ_own.at[:, pl.ds(0, 4 * tile)], occ_right, occ_ss.at[1], occ_rs.at[1], {"ao": left})
    to_right.start()
    to_left.start()

    for j in (1, 2):
        b_in[j].wait()
        widen_b(j)
        regroup(wide, tile, bt, j * tile)
        spread_b(j)

    to_right.wait_recv()
    to_left.wait_recv()
    for i, (band, shift) in enumerate(((occ_left, 0), (occ_own, 0), (occ_right, -1))):
        flag = tm_ref[0, i].astype(F32)
        for j in range(5):
            k = j + shift
            if 0 <= k < band.shape[1] // tile:
                block = band[:, pl.ds(k * tile, tile)].astype(F32) * flag
                green[pl.ds(j * tile, tile), pl.ds(i * tile, tile)] = block.T.astype(BF16)
            else:
                green[pl.ds(j * tile, tile), pl.ds(i * tile, tile)] = jnp.zeros((tile, tile), BF16)

    def make_m(first, count):
        lhs_rows = pl.ds(first * tile, count * tile)

        def body(q, carry):
            pair = jnp.concatenate([b_ref[2 * q], b_ref[2 * q + 1]], axis=1)
            got = jnp.dot(green[lhs_rows, :], pair, preferred_element_type=F32).astype(BF16)
            m_buf[2 * q, lhs_rows, :] = got[:, :tile]
            m_buf[2 * q + 1, lhs_rows, :] = got[:, tile:]
            return carry

        lax.fori_loop(0, rows // 2, body, 0)

    def m_copies(j):
        cols = pl.ds(j * tile, tile)
        return (
            remote(m_buf.at[:, pl.ds((j + 2) * tile, tile), :], m_left.at[:, cols, :], m_ss.at[j], m_rs.at[j], {"ao": right}),
            remote(m_buf.at[:, cols, :], m_right.at[:, cols, :], m_ss.at[j], m_rs.at[j], {"ao": left}),
        )

    def m_both(j):
        both = m_left.at[:, pl.ds(0, 2 * tile), :]
        return remote(both, both, m_ss.at[j], m_rs.at[j], {"ao": right})

    make_m(0, 3)
    for copy in m_copies(0):
        copy.start()
    make_m(3, 1)
    for copy in m_copies(1):
        copy.start()
    make_m(4, 1)
    for copy in m_copies(2):
        copy.start()

    hear_ao(0)
    tell_ao(1)
    for j in range(3):
        m_both(j).wait_recv()

        def n_body(p, carry, j=j):
            needed = jnp.concatenate(
                [
                    m_left[p, pl.ds(j * tile, tile), :],
                    m_buf[p, pl.ds((j + 1) * tile, tile), :],
                    m_right[p, pl.ds(j * tile, tile), :],
                ],
                axis=1,
            )
            wide[pl.ds(pl.multiple_of(p * tile, tile), tile), :] = lax.dot_general(
                needed, virt[...], (((1,), (1,)), ((), ())), preferred_element_type=F32
            )
            return carry

        lax.fori_loop(0, rows, n_body, 0)
        regroup(wide, tile, nt, j * tile)
        spread_n(j)
        b_all_of(j).wait_recv()
        forward(j).start()
        if j < 2:
            hear_ao(j + 1)
        if j == 0:
            tell_ao(2)

    def chi_part(j, first, count):
        size = count * rows
        total = None
        for l in range(0, wider, 2):
            which, at = l // share, l % share
            lhs = jnp.concatenate(
                [n_all[j, pl.ds(first, count), l + k].reshape(size, tile) for k in (0, 1)], axis=1
            )
            rhs = jnp.concatenate(
                [b_all[j, which, :, at + k].reshape(n_ri * rows, tile) for k in (0, 1)], axis=1
            )
            part = lax.dot_general(lhs, rhs, (((1,), (1,)), ((), ())), preferred_element_type=F32)
            total = part if total is None else total + part
        return total

    for j in range(2):
        forwarded(j).wait_recv()

        n_arrive(j)
        acc[...] = chi_part(j, 0, half) if j == 0 else acc[...] + chi_part(j, 0, half)
    forwarded(2).wait_recv()
    to_right.wait_send()
    to_left.wait_send()
    for j in range(3):
        m_both(j).wait_send()
        b_all_of(j).wait_send()
        forward(j).wait_send()

    def panel_copy(s):
        return remote(
            done.at[pl.ds(pl.multiple_of(s * rows, rows), rows)],
            panels.at[y],
            p_ss,
            p_rs,
            {"ri": core * half + s},
        )

    def last(i, carry):
        chip = lax.rem(y + far_first(i), n_y)

        @pl.when(chip // (n_y // 2) == core)
        def _():
            s0 = 2 * lax.rem(chip, n_y // 2)

            @pl.when(chip != y)
            def _():
                n_of(2, 2 + s0 // 2, n_ss.at[2]).wait_recv()

            @pl.when(chip == y)
            def _():
                n_of(1, 2 + s0 // 2, n_ss.at[2]).wait_recv()

            at = pl.ds(pl.multiple_of(s0 * rows, 2 * rows), 2 * rows)
            done[at, :] = (acc[at, :] + chi_part(2, s0, 2)).astype(BF16)
            for s in (s0, s0 + 1):

                @pl.when(core * half + s != ri)
                def _(s=s):
                    panel_copy(s).start()

        return carry

    lax.fori_loop(0, n_y, last, 0)

    @pl.when(core == side)
    def _():
        panels[y] = done[pl.ds(pl.multiple_of(lax.rem(ri, half) * rows, rows), rows), :]

    for j in range(3):
        n_drain(j)
    def panels_of(count):
        some = done.at[pl.ds(0, count * rows)]
        return remote(some, some, p_ss, p_rs, {"ri": y * 2 + 1 - core})

    @pl.when(core != side)
    def _():
        panels_of(n_y).wait_recv()

    @pl.when(core == side)
    def _():
        panels_of(n_y - 1).wait_recv()

    own_x[x] = jnp.sum(panels[...].astype(F32), axis=0)
    for d in range(1, n_x):
        remote(own_x.at[x], own_x.at[x], x_ss, x_rs, {"ao": x_peer(d)}).start()

    def rest_of(ref, count, ss, rs, where):
        return remote(ref.at[pl.ds(0, count)], ref.at[pl.ds(0, count)], ss, rs, where)

    if n_x > 1:
        x_rest = rest_of(own_x, n_x - 1, x_ss, x_rs, {"ao": x_peer(1)})
        x_rest.wait_recv()
    own_z[z] = jnp.sum(own_x[...], axis=0).astype(BF16)
    for i in range(n_z - 1):
        step = (i + 1) // 2
        far = n_z // 2 + (step if i % 2 == 0 else -step)
        remote(own_z.at[z], own_z.at[z], z_ss, z_rs, {"ao": z_peer(far)}).start()
    z_rest = rest_of(own_z, n_z - 1, z_ss, z_rs, {"ao": z_peer(1)})
    z_rest.wait_recv()
    o_ref[...] = -jnp.sum(own_z[...].astype(F32), axis=0)

    @pl.when(core != side)
    def _():
        panels_of(half).wait_send()

    @pl.when(core == side)
    def _():
        panels_of(half - 1).wait_send()

    if n_x > 1:
        x_rest.wait_send()
    z_rest.wait_send()


def solution(mesh):
    n_ao, n_ri = mesh.shape["ao"], mesh.shape["ri"]
    n_z = 8
    n_x = n_ao // n_z

    def per_device(three_center, occ_band, virt_band, three_mask, occ_mask, virt_mask):
        rows = three_center.shape[0]
        tile = occ_band.shape[0]
        share = tile // n_ri
        size = n_ri * rows
        dma = pltpu.SemaphoreType.DMA
        vmem = pl.BlockSpec(memory_space=pltpu.VMEM)
        return pl.pallas_call(
            functools.partial(kernel, n_ao, n_ri, n_x, n_z, tile, rows),
            out_shape=pltpu.VMEM((rows, size), F32),
            in_specs=[pl.BlockSpec(memory_space=pl.ANY)] * 6,
            out_specs=vmem,
            scratch_shapes=[
                pltpu.VMEM((rows, 3 * tile, tile), BF16),
                pltpu.VMEM((tile, 5 * tile), BF16),
                pltpu.VMEM((tile, 3 * tile), BF16),
                pltpu.SMEM((1, 3), jnp.int32),
                pltpu.SMEM((1, 5), jnp.int32),
                pltpu.SMEM((1, 3), jnp.int32),
                pltpu.VMEM((rows * tile, tile), F32),
                pltpu.VMEM((3 * tile, rows, tile), BF16),
                pltpu.VMEM((tile, 5 * tile), BF16),
                pltpu.VMEM((tile, 4 * tile), BF16),
                pltpu.VMEM((tile, 4 * tile), BF16),
                pltpu.VMEM((5 * tile, 3 * tile), BF16),
                pltpu.VMEM((tile, 3 * tile), BF16),
                pltpu.VMEM((rows, 5 * tile, tile), BF16),
                pltpu.VMEM((rows, 3 * tile, tile), BF16),
                pltpu.VMEM((rows, 3 * tile, tile), BF16),
                pltpu.VMEM((3 * tile, rows, tile), BF16),
                pltpu.VMEM((3, 2, n_ri, share, rows, tile), BF16),
                pltpu.VMEM((3, n_ri // 2, 2 * share, rows, tile), BF16),
                pltpu.VMEM((size // 2, size), F32),
                pltpu.VMEM((size // 2, size), BF16),
                pltpu.VMEM((n_ri // 2, rows, size), BF16),
                pltpu.VMEM((n_x, rows, size), F32),
                pltpu.VMEM((n_z, rows, size), BF16),
                dma((8,)),
                pltpu.SemaphoreType.REGULAR((3,)),
                pltpu.SemaphoreType.REGULAR((2,)),
                pltpu.SemaphoreType.REGULAR((3,)),
                pltpu.SemaphoreType.REGULAR((2,)),
                pltpu.SemaphoreType.REGULAR,
                dma((2,)), dma((2,)),
                dma((3,)), dma((3,)),
                dma((3,)), dma((3,)),
                dma((3,)), dma((3,)),
                dma((3,)), dma((2 + n_ri // 4,)),
                dma, dma, dma, dma, dma, dma,
            ],
            compiler_params=pltpu.CompilerParams(collective_id=0, has_side_effects=True),
        )(three_center, occ_band, virt_band, three_mask, occ_mask, virt_mask)

    return jax.shard_map(
        per_device,
        mesh=mesh,
        in_specs=(P("ri", "ao", None), P("ao", None), P("ao", None), P("ao", None), P("ao", None), P("ao", None)),
        out_specs=P("ri", None),
        check_vma=False,
    )
```

```python
import functools

import jax
import jax.numpy as jnp
from jax import lax
from jax.experimental import pallas as pl
from jax.experimental.pallas import tpu as pltpu
from jax.sharding import PartitionSpec as P

MESH = pl.DeviceIdType.MESH
F32 = jnp.float32
BF16 = jnp.bfloat16


def kernel(
    n_ao, n_ri, n_x, n_z, tile, rows,
    b_hbm, occ_hbm, virt_hbm, tm_hbm, om_hbm, vm_hbm, o_ref,
    b_ref, occ_ref, virt_ref, tm_ref, om_ref, vm_ref,
    wide, bt, occ_own, occ_left, occ_right, green, virt, m_buf, m_left, m_right,
    nt, b_all, n_all, acc, done, panels, own_x, own_z,
    in_sem, up, down, z_up, z_down, x_up, occ_ss, occ_rs, m_ss, m_rs, b_ss, b_rs, f_ss, f_rs, n_ss, n_rs, p_ss, p_rs, x_ss, x_rs, z_ss, z_rs,
):
    ao = lax.axis_index("ao")
    ri = lax.axis_index("ri")
    x, z = ao // n_z, lax.rem(ao, n_z)
    y, core = ri // 2, lax.rem(ri, 2)
    n_y = n_ri // 2
    half = n_ri // 2
    side = ri // half
    right, left = lax.rem(ao + 1, n_ao), lax.rem(ao + n_ao - 1, n_ao)
    share = tile // n_ri
    wider = 2 * share

    def far_first(i):
        step = (i + 1) // 2
        return n_y // 2 + step - 2 * step * lax.rem(i, 2)

    def remote(src, dst, ss, rs, where):
        return pltpu.make_async_remote_copy(
            src_ref=src, dst_ref=dst, send_sem=ss, recv_sem=rs, device_id=where, device_id_type=MESH
        )

    def ri_peer(d):
        return lax.rem(ri + d, n_ri)

    def x_peer(d):
        return lax.rem(x + d, n_x) * n_z + z

    def z_peer(d):
        return x * n_z + lax.rem(z + d, n_z)

    b_in = [
        pltpu.make_async_copy(
            b_hbm.at[:, pl.ds(j * tile, tile), :], b_ref.at[:, pl.ds(j * tile, tile), :], in_sem.at[j]
        )
        for j in range(3)
    ]
    small_in = [
        pltpu.make_async_copy(source, target, in_sem.at[3 + i])
        for i, (source, target) in enumerate(
            ((tm_hbm, tm_ref), (om_hbm, om_ref), (vm_hbm, vm_ref), (occ_hbm, occ_ref), (virt_hbm, virt_ref))
        )
    ]
    b_in[0].start()
    small_in[0].start()

    barrier = pltpu.get_barrier_semaphore()

    def greet(where):
        pl.semaphore_signal(barrier, inc=1, device_id=where, device_id_type=MESH)

    above, below = lax.rem(y + 1, n_y), lax.rem(y + n_y - 1, n_y)
    for chip in (above, below):
        greet({"ri": chip * 2 + core})
        greet({"ri": chip * 2 + 1 - core})
    greet({"ri": y * 2 + 1 - core})
    x_beside = (1, n_x - 1) if n_x > 1 else ()
    for where in [right, left, z_peer(1), z_peer(n_z - 1)] + [x_peer(d) for d in x_beside]:
        greet({"ao": where})

    def regroup(source_rows, stride, target, lam0):
        def body(l, carry):
            target[lam0 + l] = source_rows[pl.ds(l, rows, stride=stride), :].astype(BF16)
            return carry

        lax.fori_loop(0, tile, body, 0, unroll=16)

    def widen_b(j):
        flag = tm_ref[0, j].astype(F32)

        def body(p, carry):
            wide[pl.ds(pl.multiple_of(p * tile, tile), tile), :] = (
                b_ref[p, pl.ds(j * tile, tile), :].astype(F32) * flag
            )
            return carry

        lax.fori_loop(0, rows, body, 0, unroll=2)

    small_in[0].wait()
    b_in[0].wait()
    for copy in small_in[1:] + b_in[1:]:
        copy.start()
    widen_b(0)
    regroup(wide, tile, bt, 0)

    pl.semaphore_wait(barrier, 5 + 4 + len(x_beside))

    def tell(step):
        pl.semaphore_signal(up.at[step], inc=1, device_id={"ri": above * 2 + core}, device_id_type=MESH)
        if step < 2:
            pl.semaphore_signal(down.at[step], inc=1, device_id={"ri": below * 2 + core}, device_id_type=MESH)

    def hear(step):
        pl.semaphore_wait(up.at[step], 1)
        if step < 2:
            pl.semaphore_wait(down.at[step], 1)

    def tell_ao(step):
        pl.semaphore_signal(z_up.at[step], inc=1, device_id={"ao": z_peer(1)}, device_id_type=MESH)
        if step < 2:
            pl.semaphore_signal(z_down.at[step], inc=1, device_id={"ao": z_peer(n_z - 1)}, device_id_type=MESH)
        if step == 0 and x_beside:
            pl.semaphore_signal(x_up, inc=1, device_id={"ao": x_peer(1)}, device_id_type=MESH)

    def hear_ao(step):
        pl.semaphore_wait(z_up.at[step], 1)
        if step < 2:
            pl.semaphore_wait(z_down.at[step], 1)
        if step == 0 and x_beside:
            pl.semaphore_wait(x_up, 1)

    tell(0)
    tell_ao(0)


    def b_copy(j, i):
        peer = lax.rem(y + far_first(i // 2), n_y) * 2 + lax.rem(core + 1 + i, 2)
        return remote(
            bt.at[pl.ds(pl.multiple_of(j * tile + peer * share, share), share)],
            b_all.at[j, core_of(peer), ri],
            b_ss.at[j],
            b_rs.at[j],
            {"ri": peer},
        )

    def core_of(peer):
        return lax.rem(peer, 2)

    def spread_b(j):
        def body(i, carry):
            b_copy(j, i).start()
            return carry

        lax.fori_loop(0, n_ri - 2, body, 0)
        own_b(j)

    def own_b(j):
        b_copy(j, n_ri - 2).start()
        b_all[j, core, ri] = bt[pl.ds(pl.multiple_of(j * tile + ri * share, share), share)]

    def b_all_of(j):
        rest = bt.at[pl.ds(0, (n_ri - 1) * share)]
        return remote(rest, rest, b_ss.at[j], b_rs.at[j], {"ri": y * 2 + 1 - core})

    def forward(j):
        return remote(b_all.at[j, core], b_all.at[j, core], f_ss.at[j], f_rs.at[j], {"ri": y * 2 + 1 - core})

    def forwarded(j):
        return remote(b_all.at[j, 1 - core], b_all.at[j, 1 - core], f_ss.at[j], f_rs.at[j], {"ri": y * 2 + 1 - core})

    def n_copy(j, i):
        chip = lax.rem(y + far_first(i), n_y)
        return remote(
            nt.at[pl.ds(pl.multiple_of(j * tile + chip * wider, wider), wider)],
            n_all.at[j, lax.rem(ri, half)],
            n_ss.at[j],
            n_rs.at[j if j < 2 else 2 + lax.rem(ri, half) // 2],
            {"ri": chip * 2 + side},
        )

    def spread_n(j):
        def body(i, carry):
            n_copy(j, i).start()
            return carry

        lax.fori_loop(0, n_y - 1, body, 0)

        @pl.when(core != side)
        def _():
            n_copy(j, n_y - 1).start()

        @pl.when(core == side)
        def _():
            n_all[j, lax.rem(ri, half)] = nt[pl.ds(pl.multiple_of(j * tile + y * wider, wider), wider)]

    def n_of(sources, sem, ss):
        some = nt.at[pl.ds(0, sources * wider)]
        return remote(some, some, ss, n_rs.at[sem], {"ri": y * 2 + 1 - core})

    def n_drain(j):
        @pl.when(core != side)
        def _():
            n_of(n_y, 0, n_ss.at[j]).wait_send()

        @pl.when(core == side)
        def _():
            n_of(n_y - 1, 0, n_ss.at[j]).wait_send()

    def n_arrive(j):
        @pl.when(core != side)
        def _():
            n_of(half, j, n_ss.at[j]).wait_recv()

        @pl.when(core == side)
        def _():
            n_of(half - 1, j, n_ss.at[j]).wait_recv()

    def b_by(j, steps):
        chip = lax.rem(y + steps + n_y, n_y)
        for other in (0, 1):
            peer = chip * 2 + (core if other == 0 else 1 - core)
            remote(
                bt.at[pl.ds(pl.multiple_of(j * tile + peer * share, share), share)],
                b_all.at[j, core_of(peer), ri],
                b_ss.at[j],
                b_rs.at[j],
                {"ri": peer},
            ).start()

    b_by(0, 1)
    b_by(0, -1)
    hear(0)
    tell(1)
    b_by(0, 2)
    b_by(0, -2)
    hear(1)
    tell(2)
    b_by(0, 3)
    b_by(0, -3)
    hear(2)
    b_by(0, 4)
    own_b(0)
    for copy in small_in[1:]:
        copy.wait()
    for j in range(5):
        cols = pl.ds(j * tile, tile)
        occ_own[:, cols] = (occ_ref[:, cols].astype(F32) * om_ref[0, j].astype(F32)).astype(BF16)
    for j in range(3):
        cols = pl.ds(j * tile, tile)
        virt[:, cols] = (virt_ref[:, cols].astype(F32) * vm_ref[0, j].astype(F32)).astype(BF16)

    to_right = remote(occ_own.at[:, pl.ds(tile, 4 * tile)], occ_left, occ_ss.at[0], occ_rs.at[0], {"ao": right})
    to_left = remote(occ_own.at[:, pl.ds(0, 4 * tile)], occ_right, occ_ss.at[1], occ_rs.at[1], {"ao": left})
    to_right.start()
    to_left.start()

    for j in (1, 2):
        b_in[j].wait()
        widen_b(j)
        regroup(wide, tile, bt, j * tile)
        spread_b(j)

    to_right.wait_recv()
    to_left.wait_recv()
    for i, (band, shift) in enumerate(((occ_left, 0), (occ_own, 0), (occ_right, -1))):
        flag = tm_ref[0, i].astype(F32)
        for j in range(5):
            k = j + shift
            if 0 <= k < band.shape[1] // tile:
                block = band[:, pl.ds(k * tile, tile)].astype(F32) * flag
                green[pl.ds(j * tile, tile), pl.ds(i * tile, tile)] = block.T.astype(BF16)
            else:
                green[pl.ds(j * tile, tile), pl.ds(i * tile, tile)] = jnp.zeros((tile, tile), BF16)

    def make_m(first, count):
        lhs_rows = pl.ds(first * tile, count * tile)

        def body(q, carry):
            pair = jnp.concatenate([b_ref[2 * q], b_ref[2 * q + 1]], axis=1)
            got = jnp.dot(green[lhs_rows, :], pair, preferred_element_type=F32).astype(BF16)
            m_buf[2 * q, lhs_rows, :] = got[:, :tile]
            m_buf[2 * q + 1, lhs_rows, :] = got[:, tile:]
            return carry

        lax.fori_loop(0, rows // 2, body, 0)

    def m_copies(j):
        cols = pl.ds(j * tile, tile)
        return (
            remote(m_buf.at[:, pl.ds((j + 2) * tile, tile), :], m_left.at[:, cols, :], m_ss.at[j], m_rs.at[j], {"ao": right}),
            remote(m_buf.at[:, cols, :], m_right.at[:, cols, :], m_ss.at[j], m_rs.at[j], {"ao": left}),
        )

    def m_both(j):
        both = m_left.at[:, pl.ds(0, 2 * tile), :]
        return remote(both, both, m_ss.at[j], m_rs.at[j], {"ao": right})

    make_m(0, 3)
    for copy in m_copies(0):
        copy.start()
    make_m(3, 1)
    for copy in m_copies(1):
        copy.start()
    make_m(4, 1)
    for copy in m_copies(2):
        copy.start()

    hear_ao(0)
    tell_ao(1)
    for j in range(3):
        m_both(j).wait_recv()

        def n_body(p, carry, j=j):
            needed = jnp.concatenate(
                [
                    m_left[p, pl.ds(j * tile, tile), :],
                    m_buf[p, pl.ds((j + 1) * tile, tile), :],
                    m_right[p, pl.ds(j * tile, tile), :],
                ],
                axis=1,
            )
            wide[pl.ds(pl.multiple_of(p * tile, tile), tile), :] = lax.dot_general(
                needed, virt[...], (((1,), (1,)), ((), ())), preferred_element_type=F32
            )
            return carry

        lax.fori_loop(0, rows, n_body, 0)
        regroup(wide, tile, nt, j * tile)
        spread_n(j)
        b_all_of(j).wait_recv()
        forward(j).start()
        if j < 2:
            hear_ao(j + 1)
        if j == 0:
            tell_ao(2)

    def chi_part(j, first, count):
        size = count * rows
        total = None
        for l in range(0, wider, 2):
            which, at = l // share, l % share
            lhs = jnp.concatenate(
                [n_all[j, pl.ds(first, count), l + k].reshape(size, tile) for k in (0, 1)], axis=1
            )
            rhs = jnp.concatenate(
                [b_all[j, which, :, at + k].reshape(n_ri * rows, tile) for k in (0, 1)], axis=1
            )
            part = lax.dot_general(lhs, rhs, (((1,), (1,)), ((), ())), preferred_element_type=F32)
            total = part if total is None else total + part
        return total

    for j in range(2):
        forwarded(j).wait_recv()

        n_arrive(j)
        acc[...] = chi_part(j, 0, half) if j == 0 else acc[...] + chi_part(j, 0, half)
    forwarded(2).wait_recv()
    to_right.wait_send()
    to_left.wait_send()
    for j in range(3):
        m_both(j).wait_send()
        b_all_of(j).wait_send()
        forward(j).wait_send()

    def panel_copy(s):
        return remote(
            done.at[pl.ds(pl.multiple_of(s * rows, rows), rows)],
            panels.at[y],
            p_ss,
            p_rs,
            {"ri": core * half + s},
        )

    def last(i, carry):
        chip = lax.rem(y + far_first(i), n_y)

        @pl.when(chip // (n_y // 2) == core)
        def _():
            s0 = 2 * lax.rem(chip, n_y // 2)

            @pl.when(chip != y)
            def _():
                n_of(2, 2 + s0 // 2, n_ss.at[2]).wait_recv()

            @pl.when(chip == y)
            def _():
                n_of(1, 2 + s0 // 2, n_ss.at[2]).wait_recv()

            at = pl.ds(pl.multiple_of(s0 * rows, 2 * rows), 2 * rows)
            done[at, :] = (acc[at, :] + chi_part(2, s0, 2)).astype(BF16)
            for s in (s0, s0 + 1):

                @pl.when(core * half + s != ri)
                def _(s=s):
                    panel_copy(s).start()

        return carry

    lax.fori_loop(0, n_y, last, 0)

    @pl.when(core == side)
    def _():
        panels[y] = done[pl.ds(pl.multiple_of(lax.rem(ri, half) * rows, rows), rows), :]

    for j in range(3):
        n_drain(j)
    def panels_of(count):
        some = done.at[pl.ds(0, count * rows)]
        return remote(some, some, p_ss, p_rs, {"ri": y * 2 + 1 - core})

    @pl.when(core != side)
    def _():
        panels_of(n_y).wait_recv()

    @pl.when(core == side)
    def _():
        panels_of(n_y - 1).wait_recv()

    own_x[x] = jnp.sum(panels[...].astype(F32), axis=0)
    for d in range(1, n_x):
        remote(own_x.at[x], own_x.at[x], x_ss, x_rs, {"ao": x_peer(d)}).start()

    def rest_of(ref, count, ss, rs, where):
        return remote(ref.at[pl.ds(0, count)], ref.at[pl.ds(0, count)], ss, rs, where)

    if n_x > 1:
        x_rest = rest_of(own_x, n_x - 1, x_ss, x_rs, {"ao": x_peer(1)})
        x_rest.wait_recv()
    own_z[z] = jnp.sum(own_x[...], axis=0).astype(BF16)
    for i in range(n_z - 1):
        step = (i + 1) // 2
        far = n_z // 2 + (step if i % 2 == 0 else -step)
        remote(own_z.at[z], own_z.at[z], z_ss, z_rs, {"ao": z_peer(far)}).start()
    z_rest = rest_of(own_z, n_z - 1, z_ss, z_rs, {"ao": z_peer(1)})
    z_rest.wait_recv()
    o_ref[...] = -jnp.sum(own_z[...].astype(F32), axis=0)

    @pl.when(core != side)
    def _():
        panels_of(half).wait_send()

    @pl.when(core == side)
    def _():
        panels_of(half - 1).wait_send()

    if n_x > 1:
        x_rest.wait_send()
    z_rest.wait_send()


def solution(mesh):
    n_ao, n_ri = mesh.shape["ao"], mesh.shape["ri"]
    n_z = 8
    n_x = n_ao // n_z

    def per_device(three_center, occ_band, virt_band, three_mask, occ_mask, virt_mask):
        rows = three_center.shape[0]
        tile = occ_band.shape[0]
        share = tile // n_ri
        size = n_ri * rows
        dma = pltpu.SemaphoreType.DMA
        vmem = pl.BlockSpec(memory_space=pltpu.VMEM)
        return pl.pallas_call(
            functools.partial(kernel, n_ao, n_ri, n_x, n_z, tile, rows),
            out_shape=pltpu.VMEM((rows, size), F32),
            in_specs=[pl.BlockSpec(memory_space=pl.ANY)] * 6,
            out_specs=vmem,
            scratch_shapes=[
                pltpu.VMEM((rows, 3 * tile, tile), BF16),
                pltpu.VMEM((tile, 5 * tile), BF16),
                pltpu.VMEM((tile, 3 * tile), BF16),
                pltpu.SMEM((1, 3), jnp.int32),
                pltpu.SMEM((1, 5), jnp.int32),
                pltpu.SMEM((1, 3), jnp.int32),
                pltpu.VMEM((rows * tile, tile), F32),
                pltpu.VMEM((3 * tile, rows, tile), BF16),
                pltpu.VMEM((tile, 5 * tile), BF16),
                pltpu.VMEM((tile, 4 * tile), BF16),
                pltpu.VMEM((tile, 4 * tile), BF16),
                pltpu.VMEM((5 * tile, 3 * tile), BF16),
                pltpu.VMEM((tile, 3 * tile), BF16),
                pltpu.VMEM((rows, 5 * tile, tile), BF16),
                pltpu.VMEM((rows, 3 * tile, tile), BF16),
                pltpu.VMEM((rows, 3 * tile, tile), BF16),
                pltpu.VMEM((3 * tile, rows, tile), BF16),
                pltpu.VMEM((3, 2, n_ri, share, rows, tile), BF16),
                pltpu.VMEM((3, n_ri // 2, 2 * share, rows, tile), BF16),
                pltpu.VMEM((size // 2, size), F32),
                pltpu.VMEM((size // 2, size), BF16),
                pltpu.VMEM((n_ri // 2, rows, size), BF16),
                pltpu.VMEM((n_x, rows, size), F32),
                pltpu.VMEM((n_z, rows, size), BF16),
                dma((8,)),
                pltpu.SemaphoreType.REGULAR((3,)),
                pltpu.SemaphoreType.REGULAR((2,)),
                pltpu.SemaphoreType.REGULAR((3,)),
                pltpu.SemaphoreType.REGULAR((2,)),
                pltpu.SemaphoreType.REGULAR,
                dma((2,)), dma((2,)),
                dma((3,)), dma((3,)),
                dma((3,)), dma((3,)),
                dma((3,)), dma((3,)),
                dma((3,)), dma((2 + n_ri // 4,)),
                dma, dma, dma, dma, dma, dma,
            ],
            compiler_params=pltpu.CompilerParams(collective_id=0, has_side_effects=True),
        )(three_center, occ_band, virt_band, three_mask, occ_mask, virt_mask)

    return jax.shard_map(
        per_device,
        mesh=mesh,
        in_specs=(P("ri", "ao", None), P("ao", None), P("ao", None), P("ao", None), P("ao", None), P("ao", None)),
        out_specs=P("ri", None),
        check_vma=False,
    )
```

```python
import functools

import jax
import jax.numpy as jnp
from jax import lax
from jax.experimental import pallas as pl
from jax.experimental.pallas import tpu as pltpu
from jax.sharding import PartitionSpec as P

MESH = pl.DeviceIdType.MESH
F32 = jnp.float32
BF16 = jnp.bfloat16


def kernel(
    n_ao, n_ri, n_x, n_z, tile, rows,
    b_hbm, occ_hbm, virt_hbm, tm_hbm, om_hbm, vm_hbm, o_ref,
    b_ref, occ_ref, virt_ref, tm_ref, om_ref, vm_ref,
    wide, bt, occ_own, occ_left, occ_right, green, virt, m_buf, m_left, m_right,
    nt, b_all, n_all, acc, done, panels, own_x, own_z,
    in_sem, up, down, z_up, z_down, x_up, occ_ss, occ_rs, m_ss, m_rs, b_ss, b_rs, f_ss, f_rs, n_ss, n_rs, p_ss, p_rs, x_ss, x_rs, z_ss, z_rs,
):
    ao = lax.axis_index("ao")
    ri = lax.axis_index("ri")
    x, z = ao // n_z, lax.rem(ao, n_z)
    y, core = ri // 2, lax.rem(ri, 2)
    n_y = n_ri // 2
    half = n_ri // 2
    side = ri // half
    right, left = lax.rem(ao + 1, n_ao), lax.rem(ao + n_ao - 1, n_ao)
    share = tile // n_ri
    wider = 2 * share

    def far_first(i):
        step = (i + 1) // 2
        return n_y // 2 + step - 2 * step * lax.rem(i, 2)

    def remote(src, dst, ss, rs, where):
        return pltpu.make_async_remote_copy(
            src_ref=src, dst_ref=dst, send_sem=ss, recv_sem=rs, device_id=where, device_id_type=MESH
        )

    def ri_peer(d):
        return lax.rem(ri + d, n_ri)

    def x_peer(d):
        return lax.rem(x + d, n_x) * n_z + z

    def z_peer(d):
        return x * n_z + lax.rem(z + d, n_z)

    b_in = [
        pltpu.make_async_copy(
            b_hbm.at[:, pl.ds(j * tile, tile), :], b_ref.at[:, pl.ds(j * tile, tile), :], in_sem.at[j]
        )
        for j in range(3)
    ]
    small_in = [
        pltpu.make_async_copy(source, target, in_sem.at[3 + i])
        for i, (source, target) in enumerate(
            ((tm_hbm, tm_ref), (om_hbm, om_ref), (vm_hbm, vm_ref), (occ_hbm, occ_ref), (virt_hbm, virt_ref))
        )
    ]
    half_tile = tile // 2
    b_first = [
        pltpu.make_async_copy(
            b_hbm.at[:, pl.ds(h * half_tile, half_tile), :], b_ref.at[:, pl.ds(h * half_tile, half_tile), :], sem
        )
        for h, sem in ((0, in_sem.at[0]), (1, in_sem.at[8]))
    ]
    small_in[0].start()
    for copy in b_first:
        copy.start()

    barrier = pltpu.get_barrier_semaphore()

    def greet(where):
        pl.semaphore_signal(barrier, inc=1, device_id=where, device_id_type=MESH)

    above, below = lax.rem(y + 1, n_y), lax.rem(y + n_y - 1, n_y)
    for chip in (above, below):
        greet({"ri": chip * 2 + core})
        greet({"ri": chip * 2 + 1 - core})
    greet({"ri": y * 2 + 1 - core})
    x_beside = (1, n_x - 1) if n_x > 1 else ()
    for where in [right, left, z_peer(1), z_peer(n_z - 1)] + [x_peer(d) for d in x_beside]:
        greet({"ao": where})

    def regroup(source_rows, stride, target, lam0, first=0, count=tile):
        def body(l, carry):
            target[lam0 + l] = source_rows[pl.ds(l, rows, stride=stride), :].astype(BF16)
            return carry

        lax.fori_loop(first, first + count, body, 0, unroll=16)

    def widen_b(j, first=0, count=tile):
        flag = tm_ref[0, j].astype(F32)

        def body(p, carry):
            wide[pl.ds(pl.multiple_of(p * tile + first, count), count), :] = (
                b_ref[p, pl.ds(j * tile + first, count), :].astype(F32) * flag
            )
            return carry

        lax.fori_loop(0, rows, body, 0, unroll=2)

    small_in[0].wait()
    for h in range(2):
        b_first[h].wait()
        if h == 1:
            for copy in small_in[1:] + b_in[1:]:
                copy.start()
        widen_b(0, h * half_tile, half_tile)
        regroup(wide, tile, bt, 0, h * half_tile, half_tile)

    pl.semaphore_wait(barrier, 5 + 4 + len(x_beside))

    def tell(step):
        pl.semaphore_signal(up.at[step], inc=1, device_id={"ri": above * 2 + core}, device_id_type=MESH)
        if step < 2:
            pl.semaphore_signal(down.at[step], inc=1, device_id={"ri": below * 2 + core}, device_id_type=MESH)

    def hear(step):
        pl.semaphore_wait(up.at[step], 1)
        if step < 2:
            pl.semaphore_wait(down.at[step], 1)

    def tell_ao(step):
        pl.semaphore_signal(z_up.at[step], inc=1, device_id={"ao": z_peer(1)}, device_id_type=MESH)
        if step < 2:
            pl.semaphore_signal(z_down.at[step], inc=1, device_id={"ao": z_peer(n_z - 1)}, device_id_type=MESH)
        if step == 0 and x_beside:
            pl.semaphore_signal(x_up, inc=1, device_id={"ao": x_peer(1)}, device_id_type=MESH)

    def hear_ao(step):
        pl.semaphore_wait(z_up.at[step], 1)
        if step < 2:
            pl.semaphore_wait(z_down.at[step], 1)
        if step == 0 and x_beside:
            pl.semaphore_wait(x_up, 1)

    tell(0)
    tell_ao(0)


    def b_copy(j, i):
        peer = lax.rem(y + far_first(i // 2), n_y) * 2 + lax.rem(core + 1 + i, 2)
        return remote(
            bt.at[pl.ds(pl.multiple_of(j * tile + peer * share, share), share)],
            b_all.at[j, core_of(peer), ri],
            b_ss.at[j],
            b_rs.at[j],
            {"ri": peer},
        )

    def core_of(peer):
        return lax.rem(peer, 2)

    def spread_b(j):
        def body(i, carry):
            b_copy(j, i).start()
            return carry

        lax.fori_loop(0, n_ri - 2, body, 0)
        own_b(j)

    def own_b(j):
        b_copy(j, n_ri - 2).start()
        b_all[j, core, ri] = bt[pl.ds(pl.multiple_of(j * tile + ri * share, share), share)]

    def b_all_of(j):
        rest = bt.at[pl.ds(0, (n_ri - 1) * share)]
        return remote(rest, rest, b_ss.at[j], b_rs.at[j], {"ri": y * 2 + 1 - core})

    def forward(j):
        return remote(b_all.at[j, core], b_all.at[j, core], f_ss.at[j], f_rs.at[j], {"ri": y * 2 + 1 - core})

    def forwarded(j):
        return remote(b_all.at[j, 1 - core], b_all.at[j, 1 - core], f_ss.at[j], f_rs.at[j], {"ri": y * 2 + 1 - core})

    def n_copy(j, i):
        chip = lax.rem(y + far_first(i), n_y)
        return remote(
            nt.at[pl.ds(pl.multiple_of(j * tile + chip * wider, wider), wider)],
            n_all.at[j, lax.rem(ri, half)],
            n_ss.at[j],
            n_rs.at[j if j < 2 else 2 + lax.rem(ri, half) // 2],
            {"ri": chip * 2 + side},
        )

    def spread_n(j):
        def body(i, carry):
            n_copy(j, i).start()
            return carry

        lax.fori_loop(0, n_y - 1, body, 0)

        @pl.when(core != side)
        def _():
            n_copy(j, n_y - 1).start()

        @pl.when(core == side)
        def _():
            n_all[j, lax.rem(ri, half)] = nt[pl.ds(pl.multiple_of(j * tile + y * wider, wider), wider)]

    def n_of(sources, sem, ss):
        some = nt.at[pl.ds(0, sources * wider)]
        return remote(some, some, ss, n_rs.at[sem], {"ri": y * 2 + 1 - core})

    def n_drain(j):
        @pl.when(core != side)
        def _():
            n_of(n_y, 0, n_ss.at[j]).wait_send()

        @pl.when(core == side)
        def _():
            n_of(n_y - 1, 0, n_ss.at[j]).wait_send()

    def n_arrive(j):
        @pl.when(core != side)
        def _():
            n_of(half, j, n_ss.at[j]).wait_recv()

        @pl.when(core == side)
        def _():
            n_of(half - 1, j, n_ss.at[j]).wait_recv()

    def b_by(j, steps):
        chip = lax.rem(y + steps + n_y, n_y)
        for other in (0, 1):
            peer = chip * 2 + (core if other == 0 else 1 - core)
            remote(
                bt.at[pl.ds(pl.multiple_of(j * tile + peer * share, share), share)],
                b_all.at[j, core_of(peer), ri],
                b_ss.at[j],
                b_rs.at[j],
                {"ri": peer},
            ).start()

    b_by(0, 1)
    b_by(0, -1)
    hear(0)
    tell(1)
    b_by(0, 2)
    b_by(0, -2)
    hear(1)
    tell(2)
    b_by(0, 3)
    b_by(0, -3)
    hear(2)
    b_by(0, 4)
    own_b(0)
    for copy in small_in[1:]:
        copy.wait()
    for j in range(5):
        cols = pl.ds(j * tile, tile)
        occ_own[:, cols] = (occ_ref[:, cols].astype(F32) * om_ref[0, j].astype(F32)).astype(BF16)
    for j in range(3):
        cols = pl.ds(j * tile, tile)
        virt[:, cols] = (virt_ref[:, cols].astype(F32) * vm_ref[0, j].astype(F32)).astype(BF16)

    to_right = remote(occ_own.at[:, pl.ds(tile, 4 * tile)], occ_left, occ_ss.at[0], occ_rs.at[0], {"ao": right})
    to_left = remote(occ_own.at[:, pl.ds(0, 4 * tile)], occ_right, occ_ss.at[1], occ_rs.at[1], {"ao": left})
    to_right.start()
    to_left.start()

    for j in (1, 2):
        b_in[j].wait()
        widen_b(j)
        regroup(wide, tile, bt, j * tile)
        spread_b(j)

    to_right.wait_recv()
    to_left.wait_recv()
    for i, (band, shift) in enumerate(((occ_left, 0), (occ_own, 0), (occ_right, -1))):
        flag = tm_ref[0, i].astype(F32)
        for j in range(5):
            k = j + shift
            if 0 <= k < band.shape[1] // tile:
                block = band[:, pl.ds(k * tile, tile)].astype(F32) * flag
                green[pl.ds(j * tile, tile), pl.ds(i * tile, tile)] = block.T.astype(BF16)
            else:
                green[pl.ds(j * tile, tile), pl.ds(i * tile, tile)] = jnp.zeros((tile, tile), BF16)

    def make_m(first, count):
        lhs_rows = pl.ds(first * tile, count * tile)

        def body(q, carry):
            pair = jnp.concatenate([b_ref[2 * q], b_ref[2 * q + 1]], axis=1)
            got = jnp.dot(green[lhs_rows, :], pair, preferred_element_type=F32).astype(BF16)
            m_buf[2 * q, lhs_rows, :] = got[:, :tile]
            m_buf[2 * q + 1, lhs_rows, :] = got[:, tile:]
            return carry

        lax.fori_loop(0, rows // 2, body, 0)

    def m_copies(j):
        cols = pl.ds(j * tile, tile)
        return (
            remote(m_buf.at[:, pl.ds((j + 2) * tile, tile), :], m_left.at[:, cols, :], m_ss.at[j], m_rs.at[j], {"ao": right}),
            remote(m_buf.at[:, cols, :], m_right.at[:, cols, :], m_ss.at[j], m_rs.at[j], {"ao": left}),
        )

    def m_both(j):
        both = m_left.at[:, pl.ds(0, 2 * tile), :]
        return remote(both, both, m_ss.at[j], m_rs.at[j], {"ao": right})

    make_m(0, 3)
    for copy in m_copies(0):
        copy.start()
    make_m(3, 1)
    for copy in m_copies(1):
        copy.start()
    make_m(4, 1)
    for copy in m_copies(2):
        copy.start()

    hear_ao(0)
    tell_ao(1)
    for j in range(3):
        m_both(j).wait_recv()

        def n_body(p, carry, j=j):
            needed = jnp.concatenate(
                [
                    m_left[p, pl.ds(j * tile, tile), :],
                    m_buf[p, pl.ds((j + 1) * tile, tile), :],
                    m_right[p, pl.ds(j * tile, tile), :],
                ],
                axis=1,
            )
            wide[pl.ds(pl.multiple_of(p * tile, tile), tile), :] = lax.dot_general(
                needed, virt[...], (((1,), (1,)), ((), ())), preferred_element_type=F32
            )
            return carry

        lax.fori_loop(0, rows, n_body, 0)
        regroup(wide, tile, nt, j * tile)
        spread_n(j)
        b_all_of(j).wait_recv()
        forward(j).start()
        if j < 2:
            hear_ao(j + 1)
        if j == 0:
            tell_ao(2)

    def chi_part(j, first, count):
        size = count * rows
        total = None
        for l in range(0, wider, 2):
            which, at = l // share, l % share
            lhs = jnp.concatenate(
                [n_all[j, pl.ds(first, count), l + k].reshape(size, tile) for k in (0, 1)], axis=1
            )
            rhs = jnp.concatenate(
                [b_all[j, which, :, at + k].reshape(n_ri * rows, tile) for k in (0, 1)], axis=1
            )
            part = lax.dot_general(lhs, rhs, (((1,), (1,)), ((), ())), preferred_element_type=F32)
            total = part if total is None else total + part
        return total

    for j in range(2):
        forwarded(j).wait_recv()

        n_arrive(j)
        acc[...] = chi_part(j, 0, half) if j == 0 else acc[...] + chi_part(j, 0, half)
    forwarded(2).wait_recv()
    to_right.wait_send()
    to_left.wait_send()
    for j in range(3):
        m_both(j).wait_send()
        b_all_of(j).wait_send()
        forward(j).wait_send()

    def panel_copy(s):
        return remote(
            done.at[pl.ds(pl.multiple_of(s * rows, rows), rows)],
            panels.at[y],
            p_ss,
            p_rs,
            {"ri": core * half + s},
        )

    def last(i, carry):
        chip = lax.rem(y + far_first(i), n_y)

        @pl.when(chip // (n_y // 2) == core)
        def _():
            s0 = 2 * lax.rem(chip, n_y // 2)

            @pl.when(chip != y)
            def _():
                n_of(2, 2 + s0 // 2, n_ss.at[2]).wait_recv()

            @pl.when(chip == y)
            def _():
                n_of(1, 2 + s0 // 2, n_ss.at[2]).wait_recv()

            at = pl.ds(pl.multiple_of(s0 * rows, 2 * rows), 2 * rows)
            done[at, :] = (acc[at, :] + chi_part(2, s0, 2)).astype(BF16)
            for s in (s0, s0 + 1):

                @pl.when(core * half + s != ri)
                def _(s=s):
                    panel_copy(s).start()

        return carry

    lax.fori_loop(0, n_y, last, 0)

    @pl.when(core == side)
    def _():
        panels[y] = done[pl.ds(pl.multiple_of(lax.rem(ri, half) * rows, rows), rows), :]

    for j in range(3):
        n_drain(j)
    def panels_of(count):
        some = done.at[pl.ds(0, count * rows)]
        return remote(some, some, p_ss, p_rs, {"ri": y * 2 + 1 - core})

    @pl.when(core != side)
    def _():
        panels_of(n_y).wait_recv()

    @pl.when(core == side)
    def _():
        panels_of(n_y - 1).wait_recv()

    own_x[x] = jnp.sum(panels[...].astype(F32), axis=0)
    for d in range(1, n_x):
        remote(own_x.at[x], own_x.at[x], x_ss, x_rs, {"ao": x_peer(d)}).start()

    def rest_of(ref, count, ss, rs, where):
        return remote(ref.at[pl.ds(0, count)], ref.at[pl.ds(0, count)], ss, rs, where)

    if n_x > 1:
        x_rest = rest_of(own_x, n_x - 1, x_ss, x_rs, {"ao": x_peer(1)})
        x_rest.wait_recv()
    own_z[z] = jnp.sum(own_x[...], axis=0).astype(BF16)
    for i in range(n_z - 1):
        step = (i + 1) // 2
        far = n_z // 2 + (step if i % 2 == 0 else -step)
        remote(own_z.at[z], own_z.at[z], z_ss, z_rs, {"ao": z_peer(far)}).start()
    z_rest = rest_of(own_z, n_z - 1, z_ss, z_rs, {"ao": z_peer(1)})
    z_rest.wait_recv()
    o_ref[...] = -jnp.sum(own_z[...].astype(F32), axis=0)

    @pl.when(core != side)
    def _():
        panels_of(half).wait_send()

    @pl.when(core == side)
    def _():
        panels_of(half - 1).wait_send()

    if n_x > 1:
        x_rest.wait_send()
    z_rest.wait_send()


def solution(mesh):
    n_ao, n_ri = mesh.shape["ao"], mesh.shape["ri"]
    n_z = 8
    n_x = n_ao // n_z

    def per_device(three_center, occ_band, virt_band, three_mask, occ_mask, virt_mask):
        rows = three_center.shape[0]
        tile = occ_band.shape[0]
        share = tile // n_ri
        size = n_ri * rows
        dma = pltpu.SemaphoreType.DMA
        vmem = pl.BlockSpec(memory_space=pltpu.VMEM)
        return pl.pallas_call(
            functools.partial(kernel, n_ao, n_ri, n_x, n_z, tile, rows),
            out_shape=pltpu.VMEM((rows, size), F32),
            in_specs=[pl.BlockSpec(memory_space=pl.ANY)] * 6,
            out_specs=vmem,
            scratch_shapes=[
                pltpu.VMEM((rows, 3 * tile, tile), BF16),
                pltpu.VMEM((tile, 5 * tile), BF16),
                pltpu.VMEM((tile, 3 * tile), BF16),
                pltpu.SMEM((1, 3), jnp.int32),
                pltpu.SMEM((1, 5), jnp.int32),
                pltpu.SMEM((1, 3), jnp.int32),
                pltpu.VMEM((rows * tile, tile), F32),
                pltpu.VMEM((3 * tile, rows, tile), BF16),
                pltpu.VMEM((tile, 5 * tile), BF16),
                pltpu.VMEM((tile, 4 * tile), BF16),
                pltpu.VMEM((tile, 4 * tile), BF16),
                pltpu.VMEM((5 * tile, 3 * tile), BF16),
                pltpu.VMEM((tile, 3 * tile), BF16),
                pltpu.VMEM((rows, 5 * tile, tile), BF16),
                pltpu.VMEM((rows, 3 * tile, tile), BF16),
                pltpu.VMEM((rows, 3 * tile, tile), BF16),
                pltpu.VMEM((3 * tile, rows, tile), BF16),
                pltpu.VMEM((3, 2, n_ri, share, rows, tile), BF16),
                pltpu.VMEM((3, n_ri // 2, 2 * share, rows, tile), BF16),
                pltpu.VMEM((size // 2, size), F32),
                pltpu.VMEM((size // 2, size), BF16),
                pltpu.VMEM((n_ri // 2, rows, size), BF16),
                pltpu.VMEM((n_x, rows, size), F32),
                pltpu.VMEM((n_z, rows, size), BF16),
                dma((9,)),
                pltpu.SemaphoreType.REGULAR((3,)),
                pltpu.SemaphoreType.REGULAR((2,)),
                pltpu.SemaphoreType.REGULAR((3,)),
                pltpu.SemaphoreType.REGULAR((2,)),
                pltpu.SemaphoreType.REGULAR,
                dma((2,)), dma((2,)),
                dma((3,)), dma((3,)),
                dma((3,)), dma((3,)),
                dma((3,)), dma((3,)),
                dma((3,)), dma((2 + n_ri // 4,)),
                dma, dma, dma, dma, dma, dma,
            ],
            compiler_params=pltpu.CompilerParams(collective_id=0, has_side_effects=True),
        )(three_center, occ_band, virt_band, three_mask, occ_mask, virt_mask)

    return jax.shard_map(
        per_device,
        mesh=mesh,
        in_specs=(P("ri", "ao", None), P("ao", None), P("ao", None), P("ao", None), P("ao", None), P("ao", None)),
        out_specs=P("ri", None),
        check_vma=False,
    )
```
